128 devices in a mesh: gx: 4 (over y), gy: 32 (over x, z, core).
Axes of the slice: x: 4, y: 4, z: 4, core: 2. Of those that a mesh axis runs over, the one named last changes fastest.
Arguments:
- features: bfloat16 [4, 32, 32, 8, 8, 512], P('gx', 'gy'), may hold values from -6 to 6
- occupancy: int32 [4, 32, 32, 25], P('gx', 'gy'), may hold values from 0 to 2097151, as said below
- neighbors: int32 [4, 32, 32, 27], P('gx', 'gy'), may hold values from 0 to 48, as said below
- face_lists: int32 [4, 32, 8], P('gx', 'gy'), may hold values from 0 to 31, as said below
- face_relays: int32 [4, 32, 8], P('gx', 'gy'), may hold values from 0 to 39, as said below
- send_slots: int32 [4, 32, 32, 1], P('gx', 'gy'), may hold values from -1 to 31, as said below
- receive_order: int32 [4, 32, 16], P('gx', 'gy'), may hold values from 0 to 31, as said below
- weights: bfloat16 [27, 64, 64], replicated, may hold values from -0.15625 to 0.15625
- channel_bias: float32 [64], replicated, may hold values from -3 to 3
Outputs:
- conv_out: bfloat16 [4, 32, 16, 8, 8, 512], P('gx', 'gy')
The draws below stay inside these ranges and needn't reach their ends.
Inputs may be any that keep to these rules, and one draw needn't show every extreme that they name: `occupancy`: bit k of word w of a held block is voxel 21 * w + k; bits past voxel 8 * 8 * 8 - 1 are zero; slots that hold no block have all words zero. `neighbors`: entries name pool blocks: held slots below 32, then blocks received across faces, then the zero block 48; entry 13 is the block's own slot; other held entries name occupied slots, or any slot where the device holds none. `face_lists`: entries name slots of the device that hold blocks, or any slot where the device holds none. `face_relays`: entries below 32 name occupied held slots, or any slot where the device holds none; the others name blocks received from gy neighbours. `send_slots`: device d of a gx index sends the same number c_d of items, 0 or more, to every device of that gx index, in items q < c_d, and -1 in the others; every occupied held slot is sent exactly once; in every gx index some device has c_d = 1. `receive_order`: every device receives exactly 16 used items; its rows name each of them exactly once.
All inputs are finite; a program needn't handle non-finite values.
Results may differ from the reference program's by a relative error of at most 0.001.
Values may be sent and summed in bfloat16 or wider, within the bound.
A program may use at most 128 MiB of HBM per device.

```python
import jax
import jax.numpy as jnp
import numpy as np
from jax import lax

C = 64
BS = 8
OUT_BLOCKS = 16
HOME_SLOTS = 32
PEER_SLOTS = 1
FACE = 4
WORDS = 25
POOL = 49
N_GX = 4
N_GY = 32


def block_plan(key):
    base_key = jax.random.fold_in(key, 7)
    heavy_key, token_key, order_key = jax.random.split(base_key, 3)
    heavy = jax.random.randint(heavy_key, (N_GX, 1), 0, N_GY)
    tokens = N_GY * PEER_SLOTS

    def permute_tokens(row_key):
        return jax.random.permutation(row_key, tokens).astype(jnp.int32)
    scores = jax.vmap(permute_tokens)(jax.random.split(token_key, N_GX))
    token_ids = jnp.arange(tokens, dtype=jnp.int32)
    owner = token_ids // PEER_SLOTS
    first_item = (token_ids % PEER_SLOTS == 0).astype(jnp.int32)
    adjusted = scores + tokens * (1 - first_item)[None, :]
    adjusted = jnp.where(owner[None, :] == heavy, adjusted + 2 * tokens, adjusted)
    ranks = jnp.argsort(jnp.argsort(adjusted, axis=1, stable=True), axis=1, stable=True)
    chosen = (ranks < OUT_BLOCKS - PEER_SLOTS).astype(jnp.int32)
    counts = chosen.reshape(N_GX, N_GY, PEER_SLOTS).sum(axis=2)
    counts = jnp.where(jnp.arange(N_GY, dtype=jnp.int32)[None, :] == heavy, PEER_SLOTS, counts).astype(jnp.int32)

    def permute_slots(row_key):
        return jax.random.permutation(row_key, HOME_SLOTS).astype(jnp.int32)
    values = jax.vmap(permute_slots)(jax.random.split(order_key, N_GX * N_GY)).reshape(N_GX, N_GY, HOME_SLOTS)
    inverse = jnp.argsort(values, axis=2, stable=True).astype(jnp.int32)
    return (counts, values, inverse)


def pick_live(key, inverse, counts, shape):
    upper_bound = jnp.maximum(N_GY * counts, 1)
    extra = (1,) * (len(shape) - 2)
    ranks = jax.random.randint(key, shape, 0, upper_bound.reshape(upper_bound.shape + extra))
    flat = jnp.take_along_axis(inverse, ranks.reshape(N_GX, N_GY, -1), axis=2)
    return flat.reshape(shape)


def draw_occupancy(key, part):
    counts, values, inverse = block_plan(key)
    live = values < (N_GY * counts)[..., None]
    words = jax.random.randint(jax.random.fold_in(key, 11), (N_GX, N_GY, HOME_SLOTS, WORDS), 0, 2 ** 21)
    top_bits = BS ** 3 - 21 * (WORDS - 1)
    word_limit = np.full(WORDS, 2 ** 21 - 1, dtype=np.int32)
    word_limit[-1] = 2 ** top_bits - 1
    return jnp.where(live[..., None], words & jnp.asarray(word_limit), 0).astype(jnp.int32)


def draw_neighbors(key, part):
    counts, values, inverse = block_plan(key)
    shape = (N_GX, N_GY, HOME_SLOTS, 27)
    kind = jax.random.randint(jax.random.fold_in(key, 21), shape, 0, 10)
    local = pick_live(jax.random.fold_in(key, 22), inverse, counts, shape)
    remote = HOME_SLOTS + jax.random.randint(jax.random.fold_in(key, 23), shape, 0, 4 * FACE)
    picked = jnp.where(kind < 3, local, jnp.where(kind < 9, remote, POOL - 1))
    own_slot = jnp.broadcast_to(jnp.arange(HOME_SLOTS, dtype=jnp.int32)[None, None, :, None], shape)
    center = jnp.arange(27, dtype=jnp.int32)[None, None, None, :] == 13
    return jnp.where(center, own_slot, picked).astype(jnp.int32)


def draw_face_lists(key, part):
    counts, values, inverse = block_plan(key)
    return pick_live(jax.random.fold_in(key, 31), inverse, counts, (N_GX, N_GY, 2 * FACE)).astype(jnp.int32)


def draw_face_relays(key, part):
    counts, values, inverse = block_plan(key)
    shape = (N_GX, N_GY, 2 * FACE)
    kind = jax.random.randint(jax.random.fold_in(key, 41), shape, 0, 2)
    local = pick_live(jax.random.fold_in(key, 42), inverse, counts, shape)
    remote = HOME_SLOTS + jax.random.randint(jax.random.fold_in(key, 43), shape, 0, 2 * FACE)
    return jnp.where(kind == 0, local, remote).astype(jnp.int32)


def draw_send_slots(key, part):
    counts, values, inverse = block_plan(key)
    target = jnp.arange(N_GY, dtype=jnp.int32)[None, None, :, None]
    item_index = jnp.arange(PEER_SLOTS, dtype=jnp.int32)[None, None, None, :]
    sent = counts[:, :, None, None]
    position = jnp.minimum(target * sent + item_index, HOME_SLOTS - 1)
    position = jnp.broadcast_to(position, (N_GX, N_GY, N_GY, PEER_SLOTS))
    held = jnp.take_along_axis(inverse, position.reshape(N_GX, N_GY, -1), axis=2).reshape(N_GX, N_GY, N_GY, PEER_SLOTS)
    return jnp.where(item_index < sent, held, -1).astype(jnp.int32)


def draw_receive_order(key, part):
    counts, values, inverse = block_plan(key)
    used = (jnp.arange(PEER_SLOTS, dtype=jnp.int32)[None, None, :] < counts[:, :, None]).reshape(N_GX, 1, N_GY * PEER_SLOTS)

    def permute_items(row_key):
        return jax.random.permutation(row_key, N_GY * PEER_SLOTS).astype(jnp.int32)
    scores = jax.vmap(permute_items)(jax.random.split(jax.random.fold_in(key, 51), N_GX * N_GY)).reshape(N_GX, N_GY, N_GY * PEER_SLOTS)
    adjusted = jnp.where(used, scores, scores + N_GY * PEER_SLOTS)
    return jnp.argsort(adjusted, axis=2, stable=True)[:, :, :OUT_BLOCKS].astype(jnp.int32)


def block_levels(rng, dims, cuts, least, top_value):
    def one(dim, parts):
        heights = jax.random.uniform(jax.random.fold_in(jax.random.fold_in(rng, 6), dim), (parts,), jnp.float32, least / len(cuts), top_value / len(cuts))
        return jnp.repeat(jnp.exp(heights), dims[dim] // parts).reshape((-1,) + (1,) * (len(dims) - dim - 1))

    level = one(*cuts[0])
    for cut in cuts[1:]:
        level = level * one(*cut)
    return level


def centred(rng, shape, width, bound, pieces=(), kind=jnp.bfloat16):
    values = width * jax.random.normal(rng, shape, jnp.float32)
    if pieces:
        values = values * block_levels(rng, shape, pieces, -0.22, 0.18)
    return jnp.clip(values, -bound, bound).astype(kind)


def setup_inputs(seed: int = 0) -> dict:
    streams_of = jax.random.split(jax.random.key(seed), 10)
    return {
        "features": centred(streams_of[0], (N_GX, N_GY, HOME_SLOTS, BS, BS, BS * C), 1.0, 6.0, ((0, 4), (1, 32))),
        "occupancy": draw_occupancy(jax.random.fold_in(streams_of[9], 71), 0),
        "neighbors": draw_neighbors(jax.random.fold_in(streams_of[9], 71), 0),
        "face_lists": draw_face_lists(jax.random.fold_in(streams_of[9], 71), 0),
        "face_relays": draw_face_relays(jax.random.fold_in(streams_of[9], 71), 0),
        "send_slots": draw_send_slots(jax.random.fold_in(streams_of[9], 71), 0),
        "receive_order": draw_receive_order(jax.random.fold_in(streams_of[9], 71), 0),
        "weights": centred(streams_of[7], (27, C, C), (27 * C) ** -0.5, 0.15625),
        "channel_bias": centred(streams_of[8], (C,), 0.5, 3.0, (), jnp.float32),
    }


def unpack_bits(mask_words):
    voxels = np.arange(BS ** 3)
    picked = jnp.take(mask_words, jnp.asarray(voxels // 21, dtype=jnp.int32), axis=-1)
    occupied = jnp.right_shift(picked, jnp.asarray(voxels % 21, dtype=jnp.int32)) & 1
    return occupied.reshape(mask_words.shape[:-1] + (BS, BS, BS))


def apply_mask(blocks, mask_words):
    occupied = unpack_bits(mask_words).astype(blocks.dtype)
    spread = blocks.reshape(blocks.shape[:-1] + (BS, C)) * occupied[..., None]
    return spread.reshape(blocks.shape)


def assemble(block_pool, neighbor_rows):
    bounds = ((BS - 1, BS), (0, BS), (0, 1))
    planes = []
    for depth_x in range(3):
        row_parts = []
        for depth_y in range(3):
            column_parts = []
            for depth_z in range(3):
                section = block_pool[:, bounds[depth_x][0]:bounds[depth_x][1], bounds[depth_y][0]:bounds[depth_y][1], bounds[depth_z][0] * C:bounds[depth_z][1] * C]
                column_parts.append(jnp.take(section, neighbor_rows[:, 9 * depth_x + 3 * depth_y + depth_z], axis=0))
            row_parts.append(jnp.concatenate(column_parts, axis=3))
        planes.append(jnp.concatenate(row_parts, axis=2))
    return jnp.concatenate(planes, axis=1)


def convolve(tiles, weights, channel_bias, occupied):
    block_count = tiles.shape[0]
    shaped = tiles.astype(jnp.float32).reshape(block_count, BS + 2, BS + 2, BS + 2, C)
    weights_wide = weights.astype(jnp.float32)
    summed = jnp.zeros((block_count, BS, BS, BS, C), jnp.float32)
    for depth_x in range(3):
        for depth_y in range(3):
            for depth_z in range(3):
                window = shaped[:, depth_x:depth_x + BS, depth_y:depth_y + BS, depth_z:depth_z + BS, :]
                summed = summed + jnp.einsum("nxyzi,io->nxyzo", window, weights_wide[9 * depth_x + 3 * depth_y + depth_z])
    result = (summed + channel_bias.astype(jnp.float32)) * occupied[..., None].astype(jnp.float32)
    return result.astype(jnp.bfloat16).reshape(block_count, BS, BS, BS * C)


def reference(features, occupancy, neighbors, face_lists, face_relays, send_slots, receive_order, weights, channel_bias):
    def masked_rows(index_x, index_y, chosen):
        blocks = jnp.take(features[index_x, index_y], chosen, axis=0)
        mask_words = jnp.take(occupancy[index_x, index_y], chosen, axis=0)
        return apply_mask(blocks, mask_words)

    def pool_y(index_x, index_y):
        own_rows = masked_rows(index_x, index_y, jnp.arange(HOME_SLOTS, dtype=jnp.int32))
        below = jnp.maximum(index_y - 1, 0)
        above = jnp.minimum(index_y + 1, N_GY - 1)
        lower = masked_rows(index_x, below, face_lists[index_x, below, FACE:]) * (index_y > 0).astype(own_rows.dtype)
        upper = masked_rows(index_x, above, face_lists[index_x, above, :FACE]) * (index_y < N_GY - 1).astype(own_rows.dtype)
        return jnp.concatenate([own_rows, lower, upper], axis=0)

    def device_result(index_x, index_y):
        mine = pool_y(index_x, index_y)
        left_x = jnp.maximum(index_x - 1, 0)
        right_x = jnp.minimum(index_x + 1, N_GX - 1)
        lower = jnp.take(pool_y(left_x, index_y), face_relays[left_x, index_y, FACE:], axis=0) * (index_x > 0).astype(mine.dtype)
        upper = jnp.take(pool_y(right_x, index_y), face_relays[right_x, index_y, :FACE], axis=0) * (index_x < N_GX - 1).astype(mine.dtype)
        empty_block = jnp.zeros((1,) + mine.shape[1:], mine.dtype)
        block_pool = jnp.concatenate([mine, lower, upper, empty_block], axis=0)
        tiles = assemble(block_pool, neighbors[index_x, index_y])
        occupied = unpack_bits(occupancy[index_x, index_y])
        return convolve(tiles, weights, channel_bias, occupied)

    def row_outputs(index_x):
        results = lax.map(lambda index_y: device_result(index_x, index_y), jnp.arange(N_GY, dtype=jnp.int32))
        orders = receive_order[index_x]
        source = (orders // PEER_SLOTS).astype(jnp.int32)
        item_index = (orders % PEER_SLOTS).astype(jnp.int32)
        target = jnp.arange(N_GY, dtype=jnp.int32)[:, None]
        held_slot = send_slots[index_x][source, target, item_index]
        return results[source, held_slot]

    return lax.map(row_outputs, jnp.arange(N_GX, dtype=jnp.int32))
```

```python
import jax
import jax.numpy as jnp
from jax import lax
from jax.experimental import pallas as pl
from jax.experimental.pallas import tpu as pltpu
from jax.sharding import PartitionSpec as P

C = 64
BS = 8
LANES = BS * C
HELD = 32
FACE = 4
OUT = 16
POOL = 49
BATCH = 8
WORD_BITS = 21
MESH = pl.DeviceIdType.MESH
F32 = jnp.float32
BF16 = jnp.bfloat16


def iota(shape, dim):
    return lax.broadcasted_iota(jnp.int32, shape, dim)


def occupancy_bits(words):
    slots, width = words.shape
    voxels = BS**3
    chunks = jnp.concatenate([words & 127, (words >> 7) & 127, words >> 14], axis=0)
    voxel = iota((width, voxels), 1)
    pick = ((voxel * 3121) >> 16) == iota((width, voxels), 0)
    picked = jnp.dot(
        chunks.astype(F32).astype(BF16),
        jnp.where(pick, 1.0, 0.0).astype(BF16),
        preferred_element_type=F32,
    ).astype(jnp.int32)
    v = iota((slots, voxels), 1)
    bit = v - WORD_BITS * ((v * 3121) >> 16)
    low, mid, high = picked[:slots], picked[slots : 2 * slots], picked[2 * slots :]
    chunk = jnp.where(bit < 7, low, jnp.where(bit < 14, mid, high))
    shift = bit - jnp.where(bit >= 7, 7, 0) - jnp.where(bit >= 14, 7, 0)
    return ((chunk >> shift) & 1).astype(F32)


def build_bands(w_ref, bands):
    zero = jnp.zeros((C, C), BF16)
    for d in range(3):
        for a in range(3):
            taps = [w_ref[9 * a + 3 * d + c] for c in range(3)]
            for k, rz in enumerate((1, 0, 3, 2)):
                left = taps[rz] if rz <= 2 else zero
                right = taps[rz - 1] if rz >= 1 else zero
                pair = jnp.concatenate([left, right], axis=1)
                for xo in range(2):
                    bands[d, pl.ds((a + xo) * 4 * C + k * C, C), xo * 2 * C : (xo + 1) * 2 * C] = pair
        blank = jnp.zeros((4 * C, 2 * C), BF16)
        bands[d, 0 : 4 * C, 2 * C : 4 * C] = blank
        bands[d, 12 * C : 16 * C, 0 : 2 * C] = blank


def kernel(
    face_ref, relay_ref, send_ref, order_ref, nbr_ref, occ_ref, feat_ref, w_ref, bias_ref,
    out_ref,
    raw, pool, mask, bits, tiles, bands, outbox, inbox, fs_y, fr_y, fs_x, fr_x,
    raw_sem, ys, yr, xs, xr, ss, rs,
):
    gx = lax.axis_index("gx")
    gy = lax.axis_index("gy")
    n_gx = lax.axis_size("gx")
    n_gy = lax.axis_size("gy")
    up_y, down_y = lax.rem(gy + 1, n_gy), lax.rem(gy + n_gy - 1, n_gy)
    up_x, down_x = lax.rem(gx + 1, n_gx), lax.rem(gx + n_gx - 1, n_gx)

    barrier = pltpu.get_barrier_semaphore()

    def greet(k, carry):
        pl.semaphore_signal(barrier, inc=1, device_id=(gx, lax.rem(gy + k, n_gy)), device_id_type=MESH)
        return carry

    lax.fori_loop(1, n_gy, greet, 0)
    for other in (up_x, down_x):
        pl.semaphore_signal(barrier, inc=1, device_id=(other, gy), device_id_type=MESH)

    loads = []
    for g in range(4):
        load = pltpu.make_async_copy(feat_ref.at[pl.ds(8 * g, 8)], raw.at[pl.ds(8 * g, 8)], raw_sem.at[g])
        load.start()
        loads.append(load)

    bits[...] = occupancy_bits(occ_ref[...])
    rows = BS * BS
    own_row = jnp.where((iota((rows, LANES), 1) >> 3) == iota((rows, LANES), 0), 1.0, 0.0)
    spread = jnp.where((iota((LANES, LANES), 0) & 7) == (iota((LANES, LANES), 1) >> 6), 1.0, 0.0).astype(BF16)

    def mask_group(g, carry):
        picked = jnp.concatenate([bits[pl.ds(4 * g + i, 1), :] * own_row for i in range(4)], axis=0)
        wide = jnp.dot(picked.astype(BF16), spread, preferred_element_type=F32)
        wide = wide.reshape(4, BS, BS, LANES)
        mask[pl.ds(4 * g, 4)] = wide
        pool[pl.ds(4 * g, 4)] = raw[pl.ds(4 * g, 4)].astype(F32) * wide
        return carry

    for load in loads:
        load.wait()
    lax.fori_loop(0, HELD // 4, mask_group, 0)

    def pick_faces(t, carry):
        fs_y[t] = pool[face_ref[t]].astype(BF16)
        return carry

    lax.fori_loop(0, 2 * FACE, pick_faces, 0)
    pl.semaphore_wait(barrier, n_gy + 1)

    def exchange(src, dst, send, recv, up, down):
        copies = [
            pltpu.make_async_remote_copy(
                src_ref=src.at[pl.ds(FACE, FACE)], dst_ref=dst.at[pl.ds(0, FACE)],
                send_sem=send.at[0], recv_sem=recv.at[0], device_id=up, device_id_type=MESH),
            pltpu.make_async_remote_copy(
                src_ref=src.at[pl.ds(0, FACE)], dst_ref=dst.at[pl.ds(FACE, FACE)],
                send_sem=send.at[1], recv_sem=recv.at[1], device_id=down, device_id_type=MESH),
        ]
        for copy in copies:
            copy.start()
        return copies

    y_copies = exchange(fs_y, fr_y, ys, yr, (gx, up_y), (gx, down_y))
    pool[POOL - 1] = jnp.zeros((BS, BS, LANES), F32)
    for copy in y_copies:
        copy.wait_recv()
    low_y = jnp.where(gy > 0, 1.0, 0.0).astype(F32)
    high_y = jnp.where(gy < n_gy - 1, 1.0, 0.0).astype(F32)

    def take_y(t, carry):
        pool[HELD + t] = fr_y[t].astype(F32) * low_y
        pool[HELD + FACE + t] = fr_y[FACE + t].astype(F32) * high_y
        return carry

    lax.fori_loop(0, FACE, take_y, 0)

    def pick_relays(t, carry):
        fs_x[t] = pool[relay_ref[t]].astype(BF16)
        return carry

    lax.fori_loop(0, 2 * FACE, pick_relays, 0)
    x_copies = exchange(fs_x, fr_x, xs, xr, (up_x, gy), (down_x, gy))
    build_bands(w_ref, bands)
    for copy in x_copies:
        copy.wait_recv()
    low_x = jnp.where(gx > 0, 1.0, 0.0).astype(F32)
    high_x = jnp.where(gx < n_gx - 1, 1.0, 0.0).astype(F32)

    def take_x(t, carry):
        pool[HELD + 2 * FACE + t] = fr_x[t].astype(F32) * low_x
        pool[HELD + 3 * FACE + t] = fr_x[FACE + t].astype(F32) * high_x
        return carry

    lax.fori_loop(0, FACE, take_x, 0)

    my_x, my_z, my_core = gy // 8, lax.rem(gy // 2, 4), lax.rem(gy, 2)

    def peer(g, i, sign):
        dz, dc = i // 2, i % 2
        dx = lax.rem(g + dz, 4)
        x = lax.rem(my_x + sign * dx + 4, 4)
        z = lax.rem(my_z + sign * dz + 4, 4)
        return 8 * x + 2 * z + lax.rem(my_core + dc, 2)

    half = 2 * C
    low_half = iota((BS, half), 1) < C
    first_row = iota((BS, half), 0) == 0
    last_row = iota((BS, half), 0) == BS - 1
    bias = jnp.concatenate([bias_ref[...], bias_ref[...]], axis=1)

    def block_rows(slot, ox, x):
        views = []
        for oy in range(3):
            around = [nbr_ref[slot, 9 * ox + 3 * oy + oz] for oz in range(3)]
            parts = [pool[around[0], x, :, 3 * half : 4 * half]]
            parts += [pool[around[1], x, :, t * half : (t + 1) * half] for t in range(4)]
            parts += [pool[around[2], x, :, 0:half]]
            views.append([jnp.where(low_half, parts[t + 1], parts[t]) for t in range(5)])
        before, here, after = views
        return (
            [jnp.where(last_row, b, h) for b, h in zip(before, here)],
            here,
            [jnp.where(first_row, a, h) for a, h in zip(after, here)],
        )

    def batch(g, carry):
        slots = [jnp.maximum(send_ref[peer(g, i, 1)], 0) for i in range(BATCH)]

        def assemble(pair, inner):
            two = [jnp.maximum(send_ref[peer_pair(g, pair, i)], 0) for i in range(2)]
            for xx in range(BS + 2):
                ox = 0 if xx == 0 else (2 if xx == BS + 1 else 1)
                x = (xx - 1) % BS
                first, second = block_rows(two[0], ox, x), block_rows(two[1], ox, x)
                for d in range(3):
                    for t in range(5):
                        joined = jnp.concatenate([first[d][t], second[d][t]], axis=0)
                        tiles[d, xx % 2, xx // 2, pl.ds(pl.multiple_of(16 * pair, 16), 16), t * half : (t + 1) * half] = (
                            joined.astype(BF16)
                        )
            return inner

        def peer_pair(g, pair, i):
            dx = lax.rem(g + pair, 4)
            x = lax.rem(my_x + dx, 4)
            z = lax.rem(my_z + pair, 4)
            return 8 * x + 2 * z + lax.rem(my_core + i, 2)

        lax.fori_loop(0, BATCH // 2, assemble, 0)

        def columns(q, inner):
            lanes = pl.ds(pl.multiple_of(half * q, half), 2 * half)
            sums = []
            for d in range(3):
                window = jnp.concatenate(
                    [
                        tiles[d, j % 2, j // 2 : j // 2 + 4, :, lanes].reshape(4 * BATCH * BS, 2 * half)
                        for j in range(4)
                    ],
                    axis=1,
                )
                product = jnp.dot(window, bands[d], preferred_element_type=F32)
                sums.append(product.reshape(4 * BATCH, BS, 4 * C))
            total = sums[1] + pltpu.roll(sums[0], 1, axis=1) + pltpu.roll(sums[2], BS - 1, axis=1)
            at = pl.ds(pl.multiple_of(half * q, half), half)
            for p in range(4):
                for b in range(BATCH):
                    for xo in range(2):
                        part = total[p * BATCH + b, :, xo * half : (xo + 1) * half] + bias
                        part = part * mask[slots[b], 2 * p + xo, :, at]
                        outbox[BATCH * g + b, 2 * p + xo, :, at] = part.astype(BF16)
            return inner

        lax.fori_loop(0, 4, columns, 0)

        for i in range(BATCH):
            def send(i=i):
                move(g, i).start()

            if i == 0:
                pl.when(g > 0)(send)
            else:
                send()
        return carry

    def move(g, i):
        k = BATCH * g + i
        return pltpu.make_async_remote_copy(
            src_ref=outbox.at[k], dst_ref=inbox.at[gy], send_sem=ss.at[k], recv_sem=rs.at[k],
            device_id=(gx, peer(g, i, 1)), device_id_type=MESH)

    def arrival(g, i):
        k = BATCH * g + i
        source = peer(g, i, -1)
        return pltpu.make_async_remote_copy(
            src_ref=outbox.at[k], dst_ref=inbox.at[source], send_sem=ss.at[k], recv_sem=rs.at[k],
            device_id=(gx, source), device_id_type=MESH)

    lax.fori_loop(0, HELD // BATCH, batch, 0)
    inbox[gy] = outbox[0]
    for copy in y_copies + x_copies:
        copy.wait_send()

    def collect(g, carry):
        for i in range(BATCH):
            def wait(i=i):
                move(g, i).wait_send()
                arrival(g, i).wait_recv()

            if i == 0:
                pl.when(g > 0)(wait)
            else:
                wait()
        return carry

    lax.fori_loop(0, HELD // BATCH, collect, 0)

    def place(r, carry):
        out_ref[r] = inbox[order_ref[r]]
        return carry

    lax.fori_loop(0, OUT, place, 0)


def on_device(features, occupancy, neighbors, face_lists, face_relays, send_slots, receive_order, weights, channel_bias):
    block = (BS, BS, LANES)
    smem = pl.BlockSpec(memory_space=pltpu.SMEM)
    vmem = pl.BlockSpec(memory_space=pltpu.VMEM)
    out = pl.pallas_call(
        kernel,
        out_shape=jax.ShapeDtypeStruct((OUT,) + block, BF16),
        in_specs=[smem] * 5 + [vmem, pl.BlockSpec(memory_space=pl.ANY), vmem, vmem],
        out_specs=vmem,
        scratch_shapes=[
            pltpu.VMEM((HELD,) + block, BF16),
            pltpu.VMEM((POOL,) + block, F32),
            pltpu.VMEM((HELD,) + block, F32),
            pltpu.VMEM((HELD, LANES), F32),
            pltpu.VMEM((3, 2, 5, BATCH * BS, LANES + 2 * C), BF16),
            pltpu.VMEM((3, 16 * C, 4 * C), BF16),
            pltpu.VMEM((HELD,) + block, BF16),
            pltpu.VMEM((HELD,) + block, BF16),
            pltpu.VMEM((2 * FACE,) + block, BF16),
            pltpu.VMEM((2 * FACE,) + block, BF16),
            pltpu.VMEM((2 * FACE,) + block, BF16),
            pltpu.VMEM((2 * FACE,) + block, BF16),
            pltpu.SemaphoreType.DMA((4,)),
            pltpu.SemaphoreType.DMA((2,)),
            pltpu.SemaphoreType.DMA((2,)),
            pltpu.SemaphoreType.DMA((2,)),
            pltpu.SemaphoreType.DMA((2,)),
            pltpu.SemaphoreType.DMA((HELD,)),
            pltpu.SemaphoreType.DMA((HELD,)),
        ],
        compiler_params=pltpu.CompilerParams(
            collective_id=0, has_side_effects=True, vmem_limit_bytes=48 << 20
        ),
    )(
        face_lists[0, 0],
        face_relays[0, 0],
        send_slots[0, 0, :, 0],
        receive_order[0, 0],
        neighbors[0, 0],
        occupancy[0, 0],
        features[0, 0],
        weights,
        channel_bias.reshape(1, C),
    )
    return out[None, None]


def solution(mesh):
    in_specs = (
        P("gx", "gy", None, None, None, None),
        P("gx", "gy", None, None),
        P("gx", "gy", None, None),
        P("gx", "gy", None),
        P("gx", "gy", None),
        P("gx", "gy", None, None),
        P("gx", "gy", None),
        P(),
        P(),
    )
    out_specs = P("gx", "gy", None, None, None, None)
    return jax.shard_map(
        on_device, mesh=mesh, in_specs=in_specs, out_specs=out_specs, check_vma=False
    )
```

```python
import jax
import jax.numpy as jnp
from jax import lax
from jax.experimental import pallas as pl
from jax.experimental.pallas import tpu as pltpu
from jax.sharding import PartitionSpec as P

C = 64
BS = 8
LANES = BS * C
HELD = 32
FACE = 4
OUT = 16
POOL = 49
BATCH = 8
WORD_BITS = 21
MESH = pl.DeviceIdType.MESH
F32 = jnp.float32
BF16 = jnp.bfloat16


def iota(shape, dim):
    return lax.broadcasted_iota(jnp.int32, shape, dim)


def occupancy_bits(words):
    width, slots = words.shape
    voxels = BS**3
    chunks = jnp.concatenate([words & 127, (words >> 7) & 127, words >> 14], axis=1)
    voxel = iota((width, voxels), 1)
    pick = ((voxel * 3121) >> 16) == iota((width, voxels), 0)
    picked = lax.dot_general(
        chunks.astype(F32).astype(BF16),
        jnp.where(pick, 1.0, 0.0).astype(BF16),
        (((0,), (0,)), ((), ())),
        preferred_element_type=F32,
    ).astype(jnp.int32)
    v = iota((slots, voxels), 1)
    bit = v - WORD_BITS * ((v * 3121) >> 16)
    low, mid, high = picked[:slots], picked[slots : 2 * slots], picked[2 * slots :]
    chunk = jnp.where(bit < 7, low, jnp.where(bit < 14, mid, high))
    shift = bit - jnp.where(bit >= 7, 7, 0) - jnp.where(bit >= 14, 7, 0)
    return ((chunk >> shift) & 1).astype(F32)


def build_bands(w_ref, bands):
    zero = jnp.zeros((C, C), BF16)
    for d in range(3):
        for a in range(3):
            taps = [w_ref[9 * a + 3 * d + c] for c in range(3)]
            for k, rz in enumerate((1, 0, 3, 2)):
                left = taps[rz] if rz <= 2 else zero
                right = taps[rz - 1] if rz >= 1 else zero
                pair = jnp.concatenate([left, right], axis=1)
                for xo in range(2):
                    bands[d, pl.ds((a + xo) * 4 * C + k * C, C), xo * 2 * C : (xo + 1) * 2 * C] = pair
        blank = jnp.zeros((4 * C, 2 * C), BF16)
        bands[d, 0 : 4 * C, 2 * C : 4 * C] = blank
        bands[d, 12 * C : 16 * C, 0 : 2 * C] = blank


def kernel(
    face_hbm, relay_hbm, send_hbm, order_hbm, nbr_hbm, occ_hbm, feat_ref, w_hbm, bias_hbm,
    out_ref,
    face_ref, relay_ref, send_ref, order_ref, nbr_ref, occ_ref, w_ref, bias_ref, raw, pool, mask, bits, tiles, bands, outbox, inbox, fs_y, fr_y, fs_x, fr_x,
    small_sem, raw_sem, ys, yr, xs, xr, ss, rs,
):
    gx = lax.axis_index("gx")
    gy = lax.axis_index("gy")
    n_gx = lax.axis_size("gx")
    n_gy = lax.axis_size("gy")
    up_y, down_y = lax.rem(gy + 1, n_gy), lax.rem(gy + n_gy - 1, n_gy)
    up_x, down_x = lax.rem(gx + 1, n_gx), lax.rem(gx + n_gx - 1, n_gx)

    barrier = pltpu.get_barrier_semaphore()

    def greet(k, carry):
        pl.semaphore_signal(barrier, inc=1, device_id=(gx, lax.rem(gy + k, n_gy)), device_id_type=MESH)
        return carry

    lax.fori_loop(1, n_gy, greet, 0)
    for other in (up_x, down_x):
        pl.semaphore_signal(barrier, inc=1, device_id=(other, gy), device_id_type=MESH)

    small = []
    for i, (src, dst) in enumerate(
        (
            (occ_hbm, occ_ref), (face_hbm, face_ref), (relay_hbm, relay_ref), (send_hbm, send_ref),
            (order_hbm, order_ref), (nbr_hbm, nbr_ref), (w_hbm, w_ref), (bias_hbm, bias_ref),
        )
    ):
        load = pltpu.make_async_copy(src, dst, small_sem.at[i])
        load.start()
        small.append(load)
    loads = []
    for g in range(4):
        load = pltpu.make_async_copy(feat_ref.at[pl.ds(8 * g, 8)], raw.at[pl.ds(8 * g, 8)], raw_sem.at[g])
        load.start()
        loads.append(load)

    small[0].wait()
    bits[...] = occupancy_bits(occ_ref[...].reshape(occ_ref.shape[0], HELD))
    rows = BS * BS
    own_row = jnp.where((iota((rows, LANES), 1) >> 3) == iota((rows, LANES), 0), 1.0, 0.0)
    spread = jnp.where((iota((LANES, LANES), 0) & 7) == (iota((LANES, LANES), 1) >> 6), 1.0, 0.0).astype(BF16)

    def mask_group(g, carry):
        picked = jnp.concatenate([bits[pl.ds(4 * g + i, 1), :] * own_row for i in range(4)], axis=0)
        wide = jnp.dot(picked.astype(BF16), spread, preferred_element_type=F32)
        wide = wide.reshape(4, BS, BS, LANES)
        mask[pl.ds(4 * g, 4)] = wide
        pool[pl.ds(4 * g, 4)] = raw[pl.ds(4 * g, 4)].astype(F32) * wide
        return carry

    for load in loads + small[1:]:
        load.wait()
    lax.fori_loop(0, HELD // 4, mask_group, 0)

    def pick_faces(t, carry):
        fs_y[t] = pool[face_ref[0, t]].astype(BF16)
        return carry

    lax.fori_loop(0, 2 * FACE, pick_faces, 0)
    pl.semaphore_wait(barrier, n_gy + 1)

    def exchange(src, dst, send, recv, up, down):
        copies = [
            pltpu.make_async_remote_copy(
                src_ref=src.at[pl.ds(FACE, FACE)], dst_ref=dst.at[pl.ds(0, FACE)],
                send_sem=send.at[0], recv_sem=recv.at[0], device_id=up, device_id_type=MESH),
            pltpu.make_async_remote_copy(
                src_ref=src.at[pl.ds(0, FACE)], dst_ref=dst.at[pl.ds(FACE, FACE)],
                send_sem=send.at[1], recv_sem=recv.at[1], device_id=down, device_id_type=MESH),
        ]
        for copy in copies:
            copy.start()
        return copies

    y_copies = exchange(fs_y, fr_y, ys, yr, (gx, up_y), (gx, down_y))
    pool[POOL - 1] = jnp.zeros((BS, BS, LANES), F32)
    for copy in y_copies:
        copy.wait_recv()
    low_y = jnp.where(gy > 0, 1.0, 0.0).astype(F32)
    high_y = jnp.where(gy < n_gy - 1, 1.0, 0.0).astype(F32)

    def take_y(t, carry):
        pool[HELD + t] = fr_y[t].astype(F32) * low_y
        pool[HELD + FACE + t] = fr_y[FACE + t].astype(F32) * high_y
        return carry

    lax.fori_loop(0, FACE, take_y, 0)

    def pick_relays(t, carry):
        fs_x[t] = pool[relay_ref[0, t]].astype(BF16)
        return carry

    lax.fori_loop(0, 2 * FACE, pick_relays, 0)
    x_copies = exchange(fs_x, fr_x, xs, xr, (up_x, gy), (down_x, gy))
    build_bands(w_ref, bands)
    for copy in x_copies:
        copy.wait_recv()
    low_x = jnp.where(gx > 0, 1.0, 0.0).astype(F32)
    high_x = jnp.where(gx < n_gx - 1, 1.0, 0.0).astype(F32)

    def take_x(t, carry):
        pool[HELD + 2 * FACE + t] = fr_x[t].astype(F32) * low_x
        pool[HELD + 3 * FACE + t] = fr_x[FACE + t].astype(F32) * high_x
        return carry

    lax.fori_loop(0, FACE, take_x, 0)

    my_x, my_z, my_core = gy // 8, lax.rem(gy // 2, 4), lax.rem(gy, 2)

    def peer(g, i, sign):
        dz, dc = i // 2, i % 2
        dx = lax.rem(g + dz, 4)
        x = lax.rem(my_x + sign * dx + 4, 4)
        z = lax.rem(my_z + sign * dz + 4, 4)
        return 8 * x + 2 * z + lax.rem(my_core + dc, 2)

    half = 2 * C
    low_half = iota((BS, half), 1) < C
    first_row = iota((BS, half), 0) == 0
    last_row = iota((BS, half), 0) == BS - 1
    bias = jnp.concatenate([bias_ref[...], bias_ref[...]], axis=1)

    def block_rows(slot, ox, x):
        views = []
        for oy in range(3):
            around = [nbr_ref[9 * ox + 3 * oy + oz, 0, slot] for oz in range(3)]
            parts = [pool[around[0], x, :, 3 * half : 4 * half]]
            parts += [pool[around[1], x, :, t * half : (t + 1) * half] for t in range(4)]
            parts += [pool[around[2], x, :, 0:half]]
            views.append([jnp.where(low_half, parts[t + 1], parts[t]) for t in range(5)])
        before, here, after = views
        return (
            [jnp.where(last_row, b, h) for b, h in zip(before, here)],
            here,
            [jnp.where(first_row, a, h) for a, h in zip(after, here)],
        )

    def batch(g, carry):
        slots = [jnp.maximum(send_ref[0, peer(g, i, 1)], 0) for i in range(BATCH)]

        def assemble(pair, inner):
            two = [jnp.maximum(send_ref[0, peer_pair(g, pair, i)], 0) for i in range(2)]
            for xx in range(BS + 2):
                ox = 0 if xx == 0 else (2 if xx == BS + 1 else 1)
                x = (xx - 1) % BS
                first, second = block_rows(two[0], ox, x), block_rows(two[1], ox, x)
                for d in range(3):
                    for t in range(5):
                        joined = jnp.concatenate([first[d][t], second[d][t]], axis=0)
                        tiles[d, xx % 2, xx // 2, pl.ds(pl.multiple_of(16 * pair, 16), 16), t * half : (t + 1) * half] = (
                            joined.astype(BF16)
                        )
            return inner

        def peer_pair(g, pair, i):
            dx = lax.rem(g + pair, 4)
            x = lax.rem(my_x + dx, 4)
            z = lax.rem(my_z + pair, 4)
            return 8 * x + 2 * z + lax.rem(my_core + i, 2)

        lax.fori_loop(0, BATCH // 2, assemble, 0)

        def columns(q, inner):
            lanes = pl.ds(pl.multiple_of(half * q, half), 2 * half)
            sums = []
            for d in range(3):
                window = jnp.concatenate(
                    [
                        tiles[d, j % 2, j // 2 : j // 2 + 4, :, lanes].reshape(4 * BATCH * BS, 2 * half)
                        for j in range(4)
                    ],
                    axis=1,
                )
                product = jnp.dot(window, bands[d], preferred_element_type=F32)
                sums.append(product.reshape(4 * BATCH, BS, 4 * C))
            total = sums[1] + pltpu.roll(sums[0], 1, axis=1) + pltpu.roll(sums[2], BS - 1, axis=1)
            at = pl.ds(pl.multiple_of(half * q, half), half)
            for p in range(4):
                for b in range(BATCH):
                    for xo in range(2):
                        part = total[p * BATCH + b, :, xo * half : (xo + 1) * half] + bias
                        part = part * mask[slots[b], 2 * p + xo, :, at]
                        outbox[BATCH * g + b, 2 * p + xo, :, at] = part.astype(BF16)
            return inner

        lax.fori_loop(0, 4, columns, 0)

        for i in range(BATCH):
            def send(i=i):
                move(g, i).start()

            if i == 0:
                pl.when(g > 0)(send)
            else:
                send()
        return carry

    def move(g, i):
        k = BATCH * g + i
        return pltpu.make_async_remote_copy(
            src_ref=outbox.at[k], dst_ref=inbox.at[gy], send_sem=ss.at[k], recv_sem=rs.at[k],
            device_id=(gx, peer(g, i, 1)), device_id_type=MESH)

    def arrival(g, i):
        k = BATCH * g + i
        source = peer(g, i, -1)
        return pltpu.make_async_remote_copy(
            src_ref=outbox.at[k], dst_ref=inbox.at[source], send_sem=ss.at[k], recv_sem=rs.at[k],
            device_id=(gx, source), device_id_type=MESH)

    lax.fori_loop(0, HELD // BATCH, batch, 0)
    inbox[gy] = outbox[0]
    for copy in y_copies + x_copies:
        copy.wait_send()

    def collect(g, carry):
        for i in range(BATCH):
            def wait(i=i):
                move(g, i).wait_send()
                arrival(g, i).wait_recv()

            if i == 0:
                pl.when(g > 0)(wait)
            else:
                wait()
        return carry

    lax.fori_loop(0, HELD // BATCH, collect, 0)

    def place(r, carry):
        out_ref[r] = inbox[order_ref[0, r]]
        return carry

    lax.fori_loop(0, OUT, place, 0)


def on_device(features, occupancy, neighbors, face_lists, face_relays, send_slots, receive_order, weights, channel_bias):
    block = (BS, BS, LANES)
    out = pl.pallas_call(
        kernel,
        out_shape=jax.ShapeDtypeStruct((OUT,) + block, BF16),
        in_specs=[pl.BlockSpec(memory_space=pltpu.HBM)] * 9,
        out_specs=pl.BlockSpec(memory_space=pltpu.VMEM),
        scratch_shapes=[
            pltpu.SMEM((1, 2 * FACE), jnp.int32),
            pltpu.SMEM((1, 2 * FACE), jnp.int32),
            pltpu.SMEM((1, HELD), jnp.int32),
            pltpu.SMEM((1, OUT), jnp.int32),
            pltpu.SMEM((27, 1, HELD), jnp.int32),
            pltpu.VMEM((occupancy.shape[-1], 1, HELD), jnp.int32),
            pltpu.VMEM(weights.shape, BF16),
            pltpu.VMEM((1, C), F32),
            pltpu.VMEM((HELD,) + block, BF16),
            pltpu.VMEM((POOL,) + block, F32),
            pltpu.VMEM((HELD,) + block, F32),
            pltpu.VMEM((HELD, LANES), F32),
            pltpu.VMEM((3, 2, 5, BATCH * BS, LANES + 2 * C), BF16),
            pltpu.VMEM((3, 16 * C, 4 * C), BF16),
            pltpu.VMEM((HELD,) + block, BF16),
            pltpu.VMEM((HELD,) + block, BF16),
            pltpu.VMEM((2 * FACE,) + block, BF16),
            pltpu.VMEM((2 * FACE,) + block, BF16),
            pltpu.VMEM((2 * FACE,) + block, BF16),
            pltpu.VMEM((2 * FACE,) + block, BF16),
            pltpu.SemaphoreType.DMA((8,)),
            pltpu.SemaphoreType.DMA((4,)),
            pltpu.SemaphoreType.DMA((2,)),
            pltpu.SemaphoreType.DMA((2,)),
            pltpu.SemaphoreType.DMA((2,)),
            pltpu.SemaphoreType.DMA((2,)),
            pltpu.SemaphoreType.DMA((HELD,)),
            pltpu.SemaphoreType.DMA((HELD,)),
        ],
        compiler_params=pltpu.CompilerParams(
            collective_id=0, has_side_effects=True, vmem_limit_bytes=60 << 20
        ),
    )(
        face_lists[0],
        face_relays[0],
        send_slots[0, :, :, 0],
        receive_order[0],
        jnp.transpose(neighbors[0], (2, 0, 1)),
        jnp.transpose(occupancy[0], (2, 0, 1)),
        features[0, 0],
        weights,
        channel_bias.reshape(1, C),
    )
    return out[None, None]


def solution(mesh):
    in_specs = (
        P("gx", "gy", None, None, None, None),
        P("gx", "gy", None, None),
        P("gx", "gy", None, None),
        P("gx", "gy", None),
        P("gx", "gy", None),
        P("gx", "gy", None, None),
        P("gx", "gy", None),
        P(),
        P(),
    )
    out_specs = P("gx", "gy", None, None, None, None)
    return jax.shard_map(
        on_device, mesh=mesh, in_specs=in_specs, out_specs=out_specs, check_vma=False
    )
```

```python
import jax
import jax.numpy as jnp
from jax import lax
from jax.experimental import pallas as pl
from jax.experimental.pallas import tpu as pltpu
from jax.sharding import PartitionSpec as P

C = 64
BS = 8
LANES = BS * C
HELD = 32
FACE = 4
OUT = 16
POOL = 49
BATCH = 8
EARLY = 1
INNER = 15
SHELL = 20
WORD_BITS = 21
MESH = pl.DeviceIdType.MESH
F32 = jnp.float32
BF16 = jnp.bfloat16


def iota(shape, dim):
    return lax.broadcasted_iota(jnp.int32, shape, dim)


def occupancy_bits(words):
    width, slots = words.shape
    voxels = BS**3
    chunks = jnp.concatenate([words & 127, (words >> 7) & 127, words >> 14], axis=1)
    voxel = iota((width, voxels), 1)
    pick = ((voxel * 3121) >> 16) == iota((width, voxels), 0)
    picked = lax.dot_general(
        chunks.astype(F32).astype(BF16),
        jnp.where(pick, 1.0, 0.0).astype(BF16),
        (((0,), (0,)), ((), ())),
        preferred_element_type=F32,
    ).astype(jnp.int32)
    v = iota((slots, voxels), 1)
    bit = v - WORD_BITS * ((v * 3121) >> 16)
    low, mid, high = picked[:slots], picked[slots : 2 * slots], picked[2 * slots :]
    chunk = jnp.where(bit < 7, low, jnp.where(bit < 14, mid, high))
    shift = bit - jnp.where(bit >= 7, 7, 0) - jnp.where(bit >= 14, 7, 0)
    return ((chunk >> shift) & 1).astype(F32)


def build_bands(w_ref, bands, z_order, swapped):
    zero = jnp.zeros((C, C), BF16)
    for d in range(3):
        for a in range(3):
            taps = [w_ref[9 * a + 3 * d + c] for c in range(3)]
            for k, rz in enumerate(z_order):
                ends = [taps[rz] if rz <= 2 else zero, taps[rz - 1] if rz >= 1 else zero]
                pair = jnp.concatenate(ends[::-1] if swapped else ends, axis=1)
                for xo in range(2):
                    bands[d, pl.ds((a + xo) * 4 * C + k * C, C), xo * 2 * C : (xo + 1) * 2 * C] = pair
        blank = jnp.zeros((4 * C, 2 * C), BF16)
        bands[d, 0 : 4 * C, 2 * C : 4 * C] = blank
        bands[d, 12 * C : 16 * C, 0 : 2 * C] = blank


def kernel(
    face_hbm, relay_hbm, send_hbm, order_hbm, nbr_hbm, occ_hbm, feat_ref, w_hbm, bias_hbm,
    out_ref,
    face_ref, relay_ref, send_ref, order_ref, nbr_ref, occ_ref, w_ref, bias_ref, raw, pool, mask, bits,
    inner_tiles, inner_bands, tiles, bands, stage, inner_out, inner_in, shell_out, shell_in,
    fs_y, fr_y, fs_x, fr_x,
    small_sem, raw_sem, ys, yr, xs, xr, inner_ss, inner_rs, shell_ss, shell_rs,
):
    gx = lax.axis_index("gx")
    gy = lax.axis_index("gy")
    n_gx = lax.axis_size("gx")
    n_gy = lax.axis_size("gy")
    up_y, down_y = lax.rem(gy + 1, n_gy), lax.rem(gy + n_gy - 1, n_gy)
    up_x, down_x = lax.rem(gx + 1, n_gx), lax.rem(gx + n_gx - 1, n_gx)

    barrier = pltpu.get_barrier_semaphore()

    def greet(k, carry):
        pl.semaphore_signal(barrier, inc=1, device_id=(gx, lax.rem(gy + k, n_gy)), device_id_type=MESH)
        return carry

    lax.fori_loop(1, n_gy, greet, 0)
    for other in (up_x, down_x):
        pl.semaphore_signal(barrier, inc=1, device_id=(other, gy), device_id_type=MESH)

    small = []
    for i, (src, dst) in enumerate(
        (
            (occ_hbm, occ_ref), (face_hbm, face_ref), (relay_hbm, relay_ref), (send_hbm, send_ref),
            (order_hbm, order_ref), (nbr_hbm, nbr_ref), (w_hbm, w_ref), (bias_hbm, bias_ref),
        )
    ):
        load = pltpu.make_async_copy(src, dst, small_sem.at[i])
        load.start()
        small.append(load)
    loads = []
    for g in range(4):
        load = pltpu.make_async_copy(feat_ref.at[pl.ds(8 * g, 8)], raw.at[pl.ds(8 * g, 8)], raw_sem.at[g])
        load.start()
        loads.append(load)

    small[0].wait()
    bits[...] = occupancy_bits(occ_ref[...].reshape(occ_ref.shape[0], HELD))
    rows = BS * BS
    own_row = jnp.where((iota((rows, LANES), 1) >> 3) == iota((rows, LANES), 0), 1.0, 0.0)
    spread = jnp.where((iota((LANES, LANES), 0) & 7) == (iota((LANES, LANES), 1) >> 6), 1.0, 0.0).astype(BF16)

    def mask_group(g, carry):
        picked = jnp.concatenate([bits[pl.ds(4 * g + i, 1), :] * own_row for i in range(4)], axis=0)
        wide = jnp.dot(picked.astype(BF16), spread, preferred_element_type=F32)
        wide = wide.reshape(4, BS, BS, LANES)
        mask[pl.ds(4 * g, 4)] = wide
        pool[pl.ds(4 * g, 4)] = raw[pl.ds(4 * g, 4)].astype(F32) * wide
        return carry

    for load in small[1:]:
        load.wait()
    build_bands(w_ref, inner_bands, (0, 1, 2, 3), True)
    for load in loads:
        load.wait()
    lax.fori_loop(0, HELD // 4, mask_group, 0)

    def pick_faces(t, carry):
        fs_y[t] = pool[face_ref[0, t]].astype(BF16)
        return carry

    lax.fori_loop(0, 2 * FACE, pick_faces, 0)
    pl.semaphore_wait(barrier, n_gy + 1)

    def exchange(src, dst, send, recv, up, down):
        copies = [
            pltpu.make_async_remote_copy(
                src_ref=src.at[pl.ds(FACE, FACE)], dst_ref=dst.at[pl.ds(0, FACE)],
                send_sem=send.at[0], recv_sem=recv.at[0], device_id=up, device_id_type=MESH),
            pltpu.make_async_remote_copy(
                src_ref=src.at[pl.ds(0, FACE)], dst_ref=dst.at[pl.ds(FACE, FACE)],
                send_sem=send.at[1], recv_sem=recv.at[1], device_id=down, device_id_type=MESH),
        ]
        for copy in copies:
            copy.start()
        return copies

    y_copies = exchange(fs_y, fr_y, ys, yr, (gx, up_y), (gx, down_y))
    pool[POOL - 1] = jnp.zeros((BS, BS, LANES), F32)

    my_x, my_z, my_core = gy // 8, lax.rem(gy // 2, 4), lax.rem(gy, 2)

    def peer(g, dz, dc, sign):
        x = lax.rem(my_x + sign * lax.rem(g + dz, 4) + 4, 4)
        z = lax.rem(my_z + sign * dz + 4, 4)
        return 8 * x + 2 * z + lax.rem(my_core + dc, 2)

    half = 2 * C
    lane = iota((BS, half), 1)
    row = iota((BS, half), 0)
    low_half = lane < C
    first_row = row == 0
    last_row = row == BS - 1
    edge_row = first_row | last_row
    bias = jnp.concatenate([bias_ref[...], bias_ref[...]], axis=1)

    def slot_of(g, dz, dc):
        return jnp.maximum(send_ref[0, peer(g, dz, dc, 1)], 0)

    def turn(v, by):
        return pltpu.roll(v, by % BS, axis=0)

    def product(source, weight, planes, lanes):
        sums = []
        for d in range(3):
            window = jnp.concatenate(
                [
                    source(d, j % 2, j // 2, lanes).reshape(planes * BATCH * BS, 2 * half)
                    for j in range(4)
                ],
                axis=1,
            )
            part = jnp.dot(window, weight[d], preferred_element_type=F32)
            sums.append(part.reshape(planes * BATCH, BS, 4 * C))
        return sums[1] + pltpu.roll(sums[0], 1, axis=1) + pltpu.roll(sums[2], BS - 1, axis=1)

    def mover(out, into, send, recv):
        def outgoing(g, i):
            k = BATCH * g + i
            return pltpu.make_async_remote_copy(
                src_ref=out.at[k], dst_ref=into.at[gy], send_sem=send.at[k], recv_sem=recv.at[k],
                device_id=(gx, peer(g, i // 2, i % 2, 1)), device_id_type=MESH)

        def incoming(g, i):
            k = BATCH * g + i
            source = peer(g, i // 2, i % 2, -1)
            return pltpu.make_async_remote_copy(
                src_ref=out.at[k], dst_ref=into.at[source], send_sem=send.at[k], recv_sem=recv.at[k],
                device_id=(gx, source), device_id_type=MESH)

        def each(g, act):
            for i in range(BATCH):
                if i == 0:
                    pl.when(g > 0)(lambda: act(g, 0))
                else:
                    act(g, i)

        def start(g):
            each(g, lambda g, i: outgoing(g, i).start())

        def finish(g, carry):
            def wait(g, i):
                outgoing(g, i).wait_send()
                incoming(g, i).wait_recv()

            each(g, wait)
            return carry

        return start, finish

    start_inner, finish_inner = mover(inner_out, inner_in, inner_ss, inner_rs)
    start_shell, finish_shell = mover(shell_out, shell_in, shell_ss, shell_rs)

    def inner_batch(g, carry):
        def gather(pair, inner):
            two = [slot_of(g, pair, dc) for dc in range(2)]
            for x in range(BS):
                joined = jnp.concatenate([pool[two[0], x], pool[two[1], x]], axis=0)
                inner_tiles[x % 2, x // 2, pl.ds(pl.multiple_of(2 * BS * pair, 2 * BS), 2 * BS), :] = joined.astype(BF16)
            return inner

        lax.fori_loop(0, BATCH // 2, gather, 0)
        slots = [slot_of(g, i // 2, i % 2) for i in range(BATCH)]

        def columns(q, inner):
            lanes = pl.ds(pl.multiple_of(half * q, half), 2 * half)
            total = product(
                lambda d, odd, first, lanes: inner_tiles[odd, first : first + 3, :, lanes], inner_bands, 3, lanes)
            here = pl.ds(pl.multiple_of(half * q, half), half)
            above = pl.ds(pl.multiple_of(half * q + half, half), half)
            for b in range(BATCH):
                parts = []
                for x in range(6):
                    keep = jnp.where(low_half, mask[slots[b], x + 1, :, above], mask[slots[b], x + 1, :, here])
                    at = (x % 2) * half
                    parts.append((total[(x // 2) * BATCH + b, :, at : at + half] + bias) * keep)
                packed = [jnp.where(edge_row, turn(parts[3], 6 - 2 * m), parts[m]) for m in range(3)]
                for m, part in enumerate(packed + parts[4:]):
                    inner_out[BATCH * g + b, 5 * q + m] = part.astype(BF16)
            return inner

        lax.fori_loop(0, 3, columns, 0)
        start_inner(g)
        return carry

    def block_rows(slot, ox, x):
        views = []
        for oy in range(3):
            around = [nbr_ref[9 * ox + 3 * oy + oz, 0, slot] for oz in range(3)]
            parts = [pool[around[0], x, :, 3 * half : 4 * half]]
            parts += [pool[around[1], x, :, t * half : (t + 1) * half] for t in range(4)]
            parts += [pool[around[2], x, :, 0:half]]
            views.append([jnp.where(low_half, parts[t + 1], parts[t]) for t in range(5)])
        before, here, after = views
        return (
            [jnp.where(last_row, b, h) for b, h in zip(before, here)],
            here,
            [jnp.where(first_row, a, h) for a, h in zip(after, here)],
        )

    def shell_batch(g, carry):
        def assemble(pair, inner):
            two = [slot_of(g, pair, dc) for dc in range(2)]
            for xx in range(BS + 2):
                ox = 0 if xx == 0 else (2 if xx == BS + 1 else 1)
                x = (xx - 1) % BS
                first, second = block_rows(two[0], ox, x), block_rows(two[1], ox, x)
                for d in range(3):
                    for t in range(5):
                        joined = jnp.concatenate([first[d][t], second[d][t]], axis=0)
                        tiles[
                            d, xx % 2, xx // 2, pl.ds(pl.multiple_of(2 * BS * pair, 2 * BS), 2 * BS), t * half : (t + 1) * half
                        ] = joined.astype(BF16)
            return inner

        lax.fori_loop(0, BATCH // 2, assemble, 0)
        slots = [slot_of(g, i // 2, i % 2) for i in range(BATCH)]

        def columns(q, inner):
            lanes = pl.ds(pl.multiple_of(half * q, half), 2 * half)
            total = product(lambda d, odd, first, lanes: tiles[d, odd, first : first + 4, :, lanes], bands, 4, lanes)
            here = pl.ds(pl.multiple_of(half * q, half), half)
            for b in range(BATCH):
                for x in range(BS):
                    at = (x % 2) * half
                    part = total[(x // 2) * BATCH + b, :, at : at + half] + bias
                    stage[b, x, :, here] = part * mask[slots[b], x, :, here]
            return inner

        lax.fori_loop(0, 4, columns, 0)

        def pack(b, inner):
            k = BATCH * g + b
            for side, x in enumerate((0, BS - 1)):
                for t in range(4):
                    shell_out[k, 4 * side + t] = stage[b, x, :, t * half : (t + 1) * half].astype(BF16)
            for x in range(6):
                parts = [stage[b, x + 1, :, t * half : (t + 1) * half] for t in range(4)]
                shell_out[k, 8 + x] = jnp.where(low_half, parts[0], parts[3]).astype(BF16)
                packed = parts[0]
                for t in range(1, 4):
                    packed = jnp.where((row == 2 * t) | (row == 2 * t - 1), turn(parts[t], 2 * t), packed)
                shell_out[k, 14 + x] = packed.astype(BF16)
            return inner

        lax.fori_loop(0, BATCH, pack, 0)
        start_shell(g)
        return carry

    lax.fori_loop(0, EARLY, inner_batch, 0)
    for copy in y_copies:
        copy.wait_recv()
    low_y = jnp.where(gy > 0, 1.0, 0.0).astype(F32)
    high_y = jnp.where(gy < n_gy - 1, 1.0, 0.0).astype(F32)

    def take_y(t, carry):
        pool[HELD + t] = fr_y[t].astype(F32) * low_y
        pool[HELD + FACE + t] = fr_y[FACE + t].astype(F32) * high_y
        return carry

    lax.fori_loop(0, FACE, take_y, 0)

    def pick_relays(t, carry):
        fs_x[t] = pool[relay_ref[0, t]].astype(BF16)
        return carry

    lax.fori_loop(0, 2 * FACE, pick_relays, 0)
    x_copies = exchange(fs_x, fr_x, xs, xr, (up_x, gy), (down_x, gy))
    lax.fori_loop(EARLY, HELD // BATCH, inner_batch, 0)
    build_bands(w_ref, bands, (1, 0, 3, 2), False)
    for copy in x_copies:
        copy.wait_recv()
    low_x = jnp.where(gx > 0, 1.0, 0.0).astype(F32)
    high_x = jnp.where(gx < n_gx - 1, 1.0, 0.0).astype(F32)

    def take_x(t, carry):
        pool[HELD + 2 * FACE + t] = fr_x[t].astype(F32) * low_x
        pool[HELD + 3 * FACE + t] = fr_x[FACE + t].astype(F32) * high_x
        return carry

    lax.fori_loop(0, FACE, take_x, 0)
    lax.fori_loop(0, HELD // BATCH, shell_batch, 0)
    inner_in[gy] = inner_out[0]
    shell_in[gy] = shell_out[0]
    for copy in y_copies + x_copies:
        copy.wait_send()
    lax.fori_loop(0, HELD // BATCH, finish_inner, 0)
    lax.fori_loop(0, HELD // BATCH, finish_shell, 0)

    def place(r, carry):
        source = order_ref[0, r]
        for side, x in enumerate((0, BS - 1)):
            for t in range(4):
                out_ref[r, x, :, t * half : (t + 1) * half] = shell_in[source, 4 * side + t]
        arrived = [[inner_in[source, 5 * q + m].astype(F32) for m in range(5)] for q in range(3)]
        for x in range(6):
            middle = []
            for q in range(3):
                if x == 3:
                    first, second, third = arrived[q][:3]
                    middle.append(
                        jnp.where(row <= 2, turn(first, 2), jnp.where(row <= 4, turn(second, 4), turn(third, 6))))
                else:
                    middle.append(arrived[q][x if x < 3 else x - 1])
            ends = shell_in[source, 8 + x].astype(F32)
            packed = shell_in[source, 14 + x].astype(F32)
            chain = [ends] + middle + [ends]
            for t in range(4):
                inner = jnp.where(low_half, chain[t], chain[t + 1])
                whole = jnp.where(edge_row, turn(packed, -2 * t), inner)
                out_ref[r, x + 1, :, t * half : (t + 1) * half] = whole.astype(BF16)
        return carry

    lax.fori_loop(0, OUT, place, 0)


def on_device(features, occupancy, neighbors, face_lists, face_relays, send_slots, receive_order, weights, channel_bias):
    block = (BS, BS, LANES)
    out = pl.pallas_call(
        kernel,
        out_shape=jax.ShapeDtypeStruct((OUT,) + block, BF16),
        in_specs=[pl.BlockSpec(memory_space=pltpu.HBM)] * 9,
        out_specs=pl.BlockSpec(memory_space=pltpu.VMEM),
        scratch_shapes=[
            pltpu.SMEM((1, 2 * FACE), jnp.int32),
            pltpu.SMEM((1, 2 * FACE), jnp.int32),
            pltpu.SMEM((1, HELD), jnp.int32),
            pltpu.SMEM((1, OUT), jnp.int32),
            pltpu.SMEM((27, 1, HELD), jnp.int32),
            pltpu.VMEM((occupancy.shape[-1], 1, HELD), jnp.int32),
            pltpu.VMEM(weights.shape, BF16),
            pltpu.VMEM((1, C), F32),
            pltpu.VMEM((HELD,) + block, BF16),
            pltpu.VMEM((POOL,) + block, F32),
            pltpu.VMEM((HELD,) + block, F32),
            pltpu.VMEM((HELD, LANES), F32),
            pltpu.VMEM((2, 4, BATCH * BS, LANES), BF16),
            pltpu.VMEM((3, 16 * C, 4 * C), BF16),
            pltpu.VMEM((3, 2, 5, BATCH * BS, LANES + 2 * C), BF16),
            pltpu.VMEM((3, 16 * C, 4 * C), BF16),
            pltpu.VMEM((BATCH,) + block, F32),
            pltpu.VMEM((HELD, INNER, BS, 2 * C), BF16),
            pltpu.VMEM((HELD, INNER, BS, 2 * C), BF16),
            pltpu.VMEM((HELD, SHELL, BS, 2 * C), BF16),
            pltpu.VMEM((HELD, SHELL, BS, 2 * C), BF16),
            pltpu.VMEM((2 * FACE,) + block, BF16),
            pltpu.VMEM((2 * FACE,) + block, BF16),
            pltpu.VMEM((2 * FACE,) + block, BF16),
            pltpu.VMEM((2 * FACE,) + block, BF16),
            pltpu.SemaphoreType.DMA((8,)),
            pltpu.SemaphoreType.DMA((4,)),
            pltpu.SemaphoreType.DMA((2,)),
            pltpu.SemaphoreType.DMA((2,)),
            pltpu.SemaphoreType.DMA((2,)),
            pltpu.SemaphoreType.DMA((2,)),
            pltpu.SemaphoreType.DMA((HELD,)),
            pltpu.SemaphoreType.DMA((HELD,)),
            pltpu.SemaphoreType.DMA((HELD,)),
            pltpu.SemaphoreType.DMA((HELD,)),
        ],
        compiler_params=pltpu.CompilerParams(
            collective_id=0, has_side_effects=True, vmem_limit_bytes=60 << 20
        ),
    )(
        face_lists[0],
        face_relays[0],
        send_slots[0, :, :, 0],
        receive_order[0],
        jnp.transpose(neighbors[0], (2, 0, 1)),
        jnp.transpose(occupancy[0], (2, 0, 1)),
        features[0, 0],
        weights,
        channel_bias.reshape(1, C),
    )
    return out[None, None]


def solution(mesh):
    in_specs = (
        P("gx", "gy", None, None, None, None),
        P("gx", "gy", None, None),
        P("gx", "gy", None, None),
        P("gx", "gy", None),
        P("gx", "gy", None),
        P("gx", "gy", None, None),
        P("gx", "gy", None),
        P(),
        P(),
    )
    out_specs = P("gx", "gy", None, None, None, None)
    return jax.shard_map(
        on_device, mesh=mesh, in_specs=in_specs, out_specs=out_specs, check_vma=False
    )
```

```python
import jax
import jax.numpy as jnp
from jax import lax
from jax.experimental import pallas as pl
from jax.experimental.pallas import tpu as pltpu
from jax.sharding import PartitionSpec as P

C = 64
BS = 8
LANES = BS * C
HELD = 32
FACE = 4
OUT = 16
POOL = 49
BATCH = 8
EARLY = 1
GROUP = 4
INNER = 15
SHELL = 20
WORD_BITS = 21
MESH = pl.DeviceIdType.MESH
F32 = jnp.float32
BF16 = jnp.bfloat16


def iota(shape, dim):
    return lax.broadcasted_iota(jnp.int32, shape, dim)


def occupancy_bits(words):
    width, slots = words.shape
    voxels = BS**3
    chunks = jnp.concatenate([words & 127, (words >> 7) & 127, words >> 14], axis=1)
    voxel = iota((width, voxels), 1)
    pick = ((voxel * 3121) >> 16) == iota((width, voxels), 0)
    picked = lax.dot_general(
        chunks.astype(F32).astype(BF16),
        jnp.where(pick, 1.0, 0.0).astype(BF16),
        (((0,), (0,)), ((), ())),
        preferred_element_type=F32,
    ).astype(jnp.int32)
    v = iota((slots, voxels), 1)
    bit = v - WORD_BITS * ((v * 3121) >> 16)
    low, mid, high = picked[:slots], picked[slots : 2 * slots], picked[2 * slots :]
    chunk = jnp.where(bit < 7, low, jnp.where(bit < 14, mid, high))
    shift = bit - jnp.where(bit >= 7, 7, 0) - jnp.where(bit >= 14, 7, 0)
    return ((chunk >> shift) & 1).astype(F32)


def build_bands(w_ref, bands, z_order, swapped):
    zero = jnp.zeros((C, C), BF16)
    for d in range(3):
        for a in range(3):
            taps = [w_ref[9 * a + 3 * d + c] for c in range(3)]
            for k, rz in enumerate(z_order):
                ends = [taps[rz] if rz <= 2 else zero, taps[rz - 1] if rz >= 1 else zero]
                pair = jnp.concatenate(ends[::-1] if swapped else ends, axis=1)
                for xo in range(2):
                    bands[d, pl.ds((a + xo) * 4 * C + k * C, C), xo * 2 * C : (xo + 1) * 2 * C] = pair
        blank = jnp.zeros((4 * C, 2 * C), BF16)
        bands[d, 0 : 4 * C, 2 * C : 4 * C] = blank
        bands[d, 12 * C : 16 * C, 0 : 2 * C] = blank


def kernel(
    face_hbm, relay_hbm, send_hbm, order_hbm, nbr_hbm, occ_hbm, feat_ref, w_hbm, bias_hbm,
    out_ref,
    face_ref, relay_ref, send_ref, order_ref, nbr_ref, occ_ref, w_ref, bias_ref, chosen, raw, pool, mask, bits,
    inner_tiles, inner_bands, tiles, bands, stage, inner_out, inner_in, shell_out, shell_in,
    fs_y, fr_y, fs_x, fr_x,
    small_sem, raw_sem, ys, yr, xs, xr, inner_ss, inner_rs, shell_ss, shell_rs,
):
    gx = lax.axis_index("gx")
    gy = lax.axis_index("gy")
    n_gx = lax.axis_size("gx")
    n_gy = lax.axis_size("gy")
    up_y, down_y = lax.rem(gy + 1, n_gy), lax.rem(gy + n_gy - 1, n_gy)
    up_x, down_x = lax.rem(gx + 1, n_gx), lax.rem(gx + n_gx - 1, n_gx)

    barrier = pltpu.get_barrier_semaphore()

    def greet(k, carry):
        pl.semaphore_signal(barrier, inc=1, device_id=(gx, lax.rem(gy + k, n_gy)), device_id_type=MESH)
        return carry

    lax.fori_loop(1, n_gy, greet, 0)
    for other in (up_x, down_x):
        pl.semaphore_signal(barrier, inc=1, device_id=(other, gy), device_id_type=MESH)

    small = []
    for i, (src, dst) in enumerate(
        (
            (occ_hbm, occ_ref), (face_hbm, face_ref), (relay_hbm, relay_ref), (send_hbm, send_ref),
            (order_hbm, order_ref), (nbr_hbm, nbr_ref), (w_hbm, w_ref), (bias_hbm, bias_ref),
        )
    ):
        load = pltpu.make_async_copy(src, dst, small_sem.at[i])
        load.start()
        small.append(load)
    loads = []
    for g in range(4):
        load = pltpu.make_async_copy(feat_ref.at[pl.ds(8 * g, 8)], raw.at[pl.ds(8 * g, 8)], raw_sem.at[g])
        load.start()
        loads.append(load)

    small[0].wait()
    bits[...] = occupancy_bits(occ_ref[...].reshape(occ_ref.shape[0], HELD))
    rows = BS * BS
    own_row = jnp.where((iota((rows, LANES), 1) >> 3) == iota((rows, LANES), 0), 1.0, 0.0)
    spread = jnp.where((iota((LANES, LANES), 0) & 7) == (iota((LANES, LANES), 1) >> 6), 1.0, 0.0).astype(BF16)

    def mask_group(g, carry):
        picked = jnp.concatenate([bits[pl.ds(4 * g + i, 1), :] * own_row for i in range(4)], axis=0)
        wide = jnp.dot(picked.astype(BF16), spread, preferred_element_type=F32)
        wide = wide.reshape(4, BS, BS, LANES)
        mask[pl.ds(4 * g, 4)] = wide
        pool[pl.ds(4 * g, 4)] = raw[pl.ds(4 * g, 4)].astype(F32) * wide
        return carry

    for load in small[1:]:
        load.wait()
    build_bands(w_ref, inner_bands, (0, 1, 2, 3), True)
    for load in loads:
        load.wait()
    lax.fori_loop(0, HELD // 4, mask_group, 0)

    half = 2 * C
    lane = iota((BS, half), 1)
    row = iota((BS, half), 0)
    low_half = lane < C
    first_row = row == 0
    last_row = row == BS - 1
    edge_row = first_row | last_row

    def turn(v, by):
        return pltpu.roll(v, by % BS, axis=0)

    def pack_shell(source, block, into, k):
        for side, x in enumerate((0, BS - 1)):
            for t in range(4):
                into[k, 4 * side + t] = source[block, x, :, t * half : (t + 1) * half].astype(BF16)
        for x in range(6):
            parts = [source[block, x + 1, :, t * half : (t + 1) * half] for t in range(4)]
            into[k, 8 + x] = jnp.where(low_half, parts[0], parts[3]).astype(BF16)
            packed = parts[0]
            for t in range(1, 4):
                packed = jnp.where((row == 2 * t) | (row == 2 * t - 1), turn(parts[t], 2 * t), packed)
            into[k, 14 + x] = packed.astype(BF16)

    def unpack_shell(source, k, block, factor):
        for side, x in enumerate((0, BS - 1)):
            for t in range(4):
                pool[block, x, :, t * half : (t + 1) * half] = source[k, 4 * side + t].astype(F32) * factor
        for x in range(6):
            ends = source[k, 8 + x].astype(F32) * factor
            packed = source[k, 14 + x].astype(F32) * factor
            for t in range(4):
                whole = turn(packed, -2 * t)
                if t in (0, 3):
                    whole = jnp.where(edge_row, whole, ends)
                pool[block, x + 1, :, t * half : (t + 1) * half] = whole

    def pick_faces(t, carry):
        pack_shell(pool, face_ref[0, t], fs_y, t)
        return carry

    lax.fori_loop(0, 2 * FACE, pick_faces, 0)
    pl.semaphore_wait(barrier, n_gy + 1)

    def exchange(src, dst, send, recv, up, down):
        copies = [
            pltpu.make_async_remote_copy(
                src_ref=src.at[pl.ds(FACE, FACE)], dst_ref=dst.at[pl.ds(0, FACE)],
                send_sem=send.at[0], recv_sem=recv.at[0], device_id=up, device_id_type=MESH),
            pltpu.make_async_remote_copy(
                src_ref=src.at[pl.ds(0, FACE)], dst_ref=dst.at[pl.ds(FACE, FACE)],
                send_sem=send.at[1], recv_sem=recv.at[1], device_id=down, device_id_type=MESH),
        ]
        for copy in copies:
            copy.start()
        return copies

    y_copies = exchange(fs_y, fr_y, ys, yr, (gx, up_y), (gx, down_y))
    pool[POOL - 1] = jnp.zeros((BS, BS, LANES), F32)

    my_x, my_z, my_core = gy // 8, lax.rem(gy // 2, 4), lax.rem(gy, 2)

    offsets = (
        ((2, 1), (2, 3), (1, 2), (3, 2)),
        ((1, 1), (3, 3), (1, 3), (3, 1)),
        ((1, 0), (3, 0), (0, 1), (0, 3)),
        ((2, 0), (0, 2), (2, 2), (0, 0)),
    )
    x_codes = [sum(offsets[g][i][0] * 4**g for g in range(4)) for i in range(4)]
    z_codes = [sum(offsets[g][i][1] * 4**g for g in range(4)) for i in range(4)]

    def peer(g, i, dc, sign):
        power = lax.shift_left(1, 2 * g)
        dx = lax.rem(x_codes[i] // power, 4)
        dz = lax.rem(z_codes[i] // power, 4)
        x = lax.rem(my_x + sign * dx + 4, 4)
        z = lax.rem(my_z + sign * dz + 4, 4)
        return 8 * x + 2 * z + lax.rem(my_core + dc, 2)

    bias = jnp.concatenate([bias_ref[...], bias_ref[...]], axis=1)

    def slot_of(g, i, dc):
        return jnp.maximum(send_ref[0, peer(g, i, dc, 1)], 0)

    def product(source, weight, planes, groups):
        sums = []
        for d in range(3):
            window = jnp.concatenate(
                [
                    jnp.concatenate(
                        [
                            source(d, j % 2, j // 2, lanes).reshape(planes * BATCH * BS, 2 * half)
                            for j in range(4)
                        ],
                        axis=1,
                    )
                    for lanes in groups
                ],
                axis=0,
            )
            part = jnp.dot(window, weight[d], preferred_element_type=F32)
            sums.append(part.reshape(len(groups) * planes * BATCH, BS, 4 * C))
        return sums[1] + pltpu.roll(sums[0], 1, axis=1) + pltpu.roll(sums[2], BS - 1, axis=1)

    def at_lanes(tile, count):
        return pl.ds(pl.multiple_of(half * tile, half), count * half)

    def mover(out, into, send, recv):
        def outgoing(g, i):
            k = BATCH * g + i
            return pltpu.make_async_remote_copy(
                src_ref=out.at[k], dst_ref=into.at[gy], send_sem=send.at[k], recv_sem=recv.at[k],
                device_id=(gx, peer(g, i // 2, i % 2, 1)), device_id_type=MESH)

        def incoming(g, i):
            k = BATCH * g + i
            source = peer(g, i // 2, i % 2, -1)
            return pltpu.make_async_remote_copy(
                src_ref=out.at[k], dst_ref=into.at[source], send_sem=send.at[k], recv_sem=recv.at[k],
                device_id=(gx, source), device_id_type=MESH)

        def each(g, act):
            for i in range(BATCH):
                if i == BATCH - 2:
                    pl.when(g < HELD // BATCH - 1)(lambda: act(g, BATCH - 2))
                else:
                    act(g, i)

        def start(g):
            each(g, lambda g, i: outgoing(g, i).start())

        def finish(g, carry):
            def wait(g, i):
                outgoing(g, i).wait_send()
                incoming(g, i).wait_recv()

            each(g, wait)
            return carry

        return start, finish

    def choose(g, carry):
        for i in range(BATCH):
            chosen[BATCH * g + i] = slot_of(g, i // 2, i % 2)
        return carry

    lax.fori_loop(0, HELD // BATCH, choose, 0)
    start_inner, finish_inner = mover(inner_out, inner_in, inner_ss, inner_rs)
    start_shell, finish_shell = mover(shell_out, shell_in, shell_ss, shell_rs)

    def inner_batch(g, carry):
        def gather(pair, inner):
            two = [chosen[BATCH * g + 2 * pair + dc] for dc in range(2)]
            for x in range(BS):
                joined = jnp.concatenate([pool[two[0], x], pool[two[1], x]], axis=0)
                inner_tiles[x % 2, x // 2, pl.ds(pl.multiple_of(2 * BS * pair, 2 * BS), 2 * BS), :] = joined.astype(BF16)
            return inner

        lax.fori_loop(0, BATCH // 2, gather, 0)
        slots = [chosen[BATCH * g + i] for i in range(BATCH)]

        def columns(q, inner):
            total = product(
                lambda d, odd, first, lanes: inner_tiles[odd, first : first + 3, :, lanes],
                inner_bands, 3, [at_lanes(q, 2)])
            here, above = at_lanes(q, 1), at_lanes(q + 1, 1)
            for b in range(BATCH):
                parts = []
                for x in range(6):
                    keep = jnp.where(low_half, mask[slots[b], x + 1, :, above], mask[slots[b], x + 1, :, here])
                    at = (x % 2) * half
                    parts.append((total[(x // 2) * BATCH + b, :, at : at + half] + bias) * keep)
                packed = [jnp.where(edge_row, turn(parts[3], 6 - 2 * m), parts[m]) for m in range(3)]
                for m, part in enumerate(packed + parts[4:]):
                    inner_out[BATCH * g + b, 5 * q + m] = part.astype(BF16)
            return inner

        lax.fori_loop(0, 3, columns, 0)
        start_inner(g)
        return carry

    def block_rows(slot, ox, x):
        views = []
        for oy in range(3):
            around = [nbr_ref[9 * ox + 3 * oy + oz, 0, slot] for oz in range(3)]
            parts = [pool[around[0], x, :, 3 * half : 4 * half]]
            parts += [pool[around[1], x, :, t * half : (t + 1) * half] for t in range(4)]
            parts += [pool[around[2], x, :, 0:half]]
            views.append([jnp.where(low_half, parts[t + 1], parts[t]) for t in range(5)])
        before, here, after = views
        return (
            [jnp.where(last_row, b, h) for b, h in zip(before, here)],
            here,
            [jnp.where(first_row, a, h) for a, h in zip(after, here)],
        )

    def shell_batch(g, carry):
        def assemble(pair, inner):
            two = [chosen[BATCH * g + 2 * pair + dc] for dc in range(2)]
            for xx in range(BS + 2):
                ox = 0 if xx == 0 else (2 if xx == BS + 1 else 1)
                x = (xx - 1) % BS
                first, second = block_rows(two[0], ox, x), block_rows(two[1], ox, x)
                for d in range(3):
                    for t in range(5):
                        joined = jnp.concatenate([first[d][t], second[d][t]], axis=0)
                        tiles[
                            d, xx % 2, xx // 2, pl.ds(pl.multiple_of(2 * BS * pair, 2 * BS), 2 * BS), t * half : (t + 1) * half
                        ] = joined.astype(BF16)
            return inner

        lax.fori_loop(0, BATCH // 2, assemble, 0)
        slots = [chosen[BATCH * g + i] for i in range(BATCH)]

        def columns(step, inner):
            total = product(
                lambda d, odd, first, lanes: tiles[d, odd, first : first + 4, :, lanes],
                bands, 4, [at_lanes(GROUP * step + i, 2) for i in range(GROUP)])
            for i in range(GROUP):
                here = at_lanes(GROUP * step + i, 1)
                for b in range(BATCH):
                    for x in range(BS):
                        at = (x % 2) * half
                        part = total[(4 * i + x // 2) * BATCH + b, :, at : at + half] + bias
                        stage[b, x, :, here] = part * mask[slots[b], x, :, here]
            return inner

        lax.fori_loop(0, 4 // GROUP, columns, 0)

        def pack(b, inner):
            pack_shell(stage, b, shell_out, BATCH * g + b)
            return inner

        lax.fori_loop(0, BATCH, pack, 0)
        start_shell(g)
        return carry

    lax.fori_loop(0, EARLY, inner_batch, 0)
    for copy in y_copies:
        copy.wait_recv()
    low_y = jnp.where(gy > 0, 1.0, 0.0).astype(F32)
    high_y = jnp.where(gy < n_gy - 1, 1.0, 0.0).astype(F32)

    def take_y(t, carry):
        unpack_shell(fr_y, t, HELD + t, low_y)
        unpack_shell(fr_y, FACE + t, HELD + FACE + t, high_y)
        return carry

    lax.fori_loop(0, FACE, take_y, 0)

    def pick_relays(t, carry):
        pack_shell(pool, relay_ref[0, t], fs_x, t)
        return carry

    lax.fori_loop(0, 2 * FACE, pick_relays, 0)
    x_copies = exchange(fs_x, fr_x, xs, xr, (up_x, gy), (down_x, gy))
    lax.fori_loop(EARLY, HELD // BATCH, inner_batch, 0)
    build_bands(w_ref, bands, (1, 0, 3, 2), False)
    for copy in x_copies:
        copy.wait_recv()
    low_x = jnp.where(gx > 0, 1.0, 0.0).astype(F32)
    high_x = jnp.where(gx < n_gx - 1, 1.0, 0.0).astype(F32)

    def take_x(t, carry):
        unpack_shell(fr_x, t, HELD + 2 * FACE + t, low_x)
        unpack_shell(fr_x, FACE + t, HELD + 3 * FACE + t, high_x)
        return carry

    lax.fori_loop(0, FACE, take_x, 0)
    lax.fori_loop(0, HELD // BATCH, shell_batch, 0)
    inner_in[gy] = inner_out[HELD - 2]
    shell_in[gy] = shell_out[HELD - 2]
    for copy in y_copies + x_copies:
        copy.wait_send()
    lax.fori_loop(0, HELD // BATCH, finish_inner, 0)
    lax.fori_loop(0, HELD // BATCH, finish_shell, 0)

    def place(r, carry):
        source = order_ref[0, r]
        for side, x in enumerate((0, BS - 1)):
            for t in range(4):
                out_ref[r, x, :, t * half : (t + 1) * half] = shell_in[source, 4 * side + t]
        arrived = [[inner_in[source, 5 * q + m].astype(F32) for m in range(5)] for q in range(3)]
        for x in range(6):
            middle = []
            for q in range(3):
                if x == 3:
                    first, second, third = arrived[q][:3]
                    middle.append(
                        jnp.where(row <= 2, turn(first, 2), jnp.where(row <= 4, turn(second, 4), turn(third, 6))))
                else:
                    middle.append(arrived[q][x if x < 3 else x - 1])
            ends = shell_in[source, 8 + x].astype(F32)
            packed = shell_in[source, 14 + x].astype(F32)
            chain = [ends] + middle + [ends]
            for t in range(4):
                inner = jnp.where(low_half, chain[t], chain[t + 1])
                whole = jnp.where(edge_row, turn(packed, -2 * t), inner)
                out_ref[r, x + 1, :, t * half : (t + 1) * half] = whole.astype(BF16)
        return carry

    lax.fori_loop(0, OUT, place, 0)


def on_device(features, occupancy, neighbors, face_lists, face_relays, send_slots, receive_order, weights, channel_bias):
    block = (BS, BS, LANES)
    out = pl.pallas_call(
        kernel,
        out_shape=jax.ShapeDtypeStruct((OUT,) + block, BF16),
        in_specs=[pl.BlockSpec(memory_space=pltpu.HBM)] * 9,
        out_specs=pl.BlockSpec(memory_space=pltpu.VMEM),
        scratch_shapes=[
            pltpu.SMEM((1, 2 * FACE), jnp.int32),
            pltpu.SMEM((1, 2 * FACE), jnp.int32),
            pltpu.SMEM((1, HELD), jnp.int32),
            pltpu.SMEM((1, OUT), jnp.int32),
            pltpu.SMEM((27, 1, HELD), jnp.int32),
            pltpu.VMEM((occupancy.shape[-1], 1, HELD), jnp.int32),
            pltpu.VMEM(weights.shape, BF16),
            pltpu.VMEM((1, C), F32),
            pltpu.SMEM((HELD,), jnp.int32),
            pltpu.VMEM((HELD,) + block, BF16),
            pltpu.VMEM((POOL,) + block, F32),
            pltpu.VMEM((HELD,) + block, F32),
            pltpu.VMEM((HELD, LANES), F32),
            pltpu.VMEM((2, 4, BATCH * BS, LANES), BF16),
            pltpu.VMEM((3, 16 * C, 4 * C), BF16),
            pltpu.VMEM((3, 2, 5, BATCH * BS, LANES + 2 * C), BF16),
            pltpu.VMEM((3, 16 * C, 4 * C), BF16),
            pltpu.VMEM((BATCH,) + block, F32),
            pltpu.VMEM((HELD, INNER, BS, 2 * C), BF16),
            pltpu.VMEM((HELD, INNER, BS, 2 * C), BF16),
            pltpu.VMEM((HELD, SHELL, BS, 2 * C), BF16),
            pltpu.VMEM((HELD, SHELL, BS, 2 * C), BF16),
            pltpu.VMEM((2 * FACE, SHELL, BS, 2 * C), BF16),
            pltpu.VMEM((2 * FACE, SHELL, BS, 2 * C), BF16),
            pltpu.VMEM((2 * FACE, SHELL, BS, 2 * C), BF16),
            pltpu.VMEM((2 * FACE, SHELL, BS, 2 * C), BF16),
            pltpu.SemaphoreType.DMA((8,)),
            pltpu.SemaphoreType.DMA((4,)),
            pltpu.SemaphoreType.DMA((2,)),
            pltpu.SemaphoreType.DMA((2,)),
            pltpu.SemaphoreType.DMA((2,)),
            pltpu.SemaphoreType.DMA((2,)),
            pltpu.SemaphoreType.DMA((HELD,)),
            pltpu.SemaphoreType.DMA((HELD,)),
            pltpu.SemaphoreType.DMA((HELD,)),
            pltpu.SemaphoreType.DMA((HELD,)),
        ],
        compiler_params=pltpu.CompilerParams(
            collective_id=0, has_side_effects=True, vmem_limit_bytes=60 << 20
        ),
    )(
        face_lists[0],
        face_relays[0],
        send_slots[0, :, :, 0],
        receive_order[0],
        jnp.transpose(neighbors[0], (2, 0, 1)),
        jnp.transpose(occupancy[0], (2, 0, 1)),
        features[0, 0],
        weights,
        channel_bias.reshape(1, C),
    )
    return out[None, None]


def solution(mesh):
    in_specs = (
        P("gx", "gy", None, None, None, None),
        P("gx", "gy", None, None),
        P("gx", "gy", None, None),
        P("gx", "gy", None),
        P("gx", "gy", None),
        P("gx", "gy", None, None),
        P("gx", "gy", None),
        P(),
        P(),
    )
    out_specs = P("gx", "gy", None, None, None, None)
    return jax.shard_map(
        on_device, mesh=mesh, in_specs=in_specs, out_specs=out_specs, check_vma=False
    )
```

```python
import jax
import jax.numpy as jnp
from jax import lax
from jax.experimental import pallas as pl
from jax.experimental.pallas import tpu as pltpu
from jax.sharding import PartitionSpec as P

C = 64
BS = 8
LANES = BS * C
HELD = 32
FACE = 4
OUT = 16
POOL = 49
BATCH = 8
EARLY = 1
GROUP = 4
INNER = 14
SHELL = 19
WORD_BITS = 21
MESH = pl.DeviceIdType.MESH
F32 = jnp.float32
BF16 = jnp.bfloat16


def iota(shape, dim):
    return lax.broadcasted_iota(jnp.int32, shape, dim)


def occupancy_bits(words):
    width, slots = words.shape
    voxels = BS**3
    chunks = jnp.concatenate([words & 127, (words >> 7) & 127, words >> 14], axis=1)
    voxel = iota((width, voxels), 1)
    pick = ((voxel * 3121) >> 16) == iota((width, voxels), 0)
    picked = lax.dot_general(
        chunks.astype(F32).astype(BF16),
        jnp.where(pick, 1.0, 0.0).astype(BF16),
        (((0,), (0,)), ((), ())),
        preferred_element_type=F32,
    ).astype(jnp.int32)
    v = iota((slots, voxels), 1)
    bit = v - WORD_BITS * ((v * 3121) >> 16)
    low, mid, high = picked[:slots], picked[slots : 2 * slots], picked[2 * slots :]
    chunk = jnp.where(bit < 7, low, jnp.where(bit < 14, mid, high))
    shift = bit - jnp.where(bit >= 7, 7, 0) - jnp.where(bit >= 14, 7, 0)
    return ((chunk >> shift) & 1).astype(F32)


def build_bands(w_ref, bands, z_order, swapped):
    zero = jnp.zeros((C, C), BF16)
    for d in range(3):
        for a in range(3):
            taps = [w_ref[9 * a + 3 * d + c] for c in range(3)]
            for k, rz in enumerate(z_order):
                ends = [taps[rz] if rz <= 2 else zero, taps[rz - 1] if rz >= 1 else zero]
                pair = jnp.concatenate(ends[::-1] if swapped else ends, axis=1)
                for xo in range(2):
                    bands[d, pl.ds((a + xo) * 4 * C + k * C, C), xo * 2 * C : (xo + 1) * 2 * C] = pair
        blank = jnp.zeros((4 * C, 2 * C), BF16)
        bands[d, 0 : 4 * C, 2 * C : 4 * C] = blank
        bands[d, 12 * C : 16 * C, 0 : 2 * C] = blank


def kernel(
    face_hbm, relay_hbm, send_hbm, order_hbm, nbr_hbm, occ_hbm, feat_ref, w_hbm, bias_hbm,
    out_ref,
    face_ref, relay_ref, send_ref, order_ref, nbr_ref, occ_ref, w_ref, bias_ref, chosen, raw, pool, mask, bits,
    inner_tiles, inner_bands, tiles, bands, stage, inner_out, inner_in, shell_out, shell_in,
    fs_y, fr_y, fs_x, fr_x,
    small_sem, raw_sem, ys, yr, xs, xr, inner_ss, inner_rs, shell_ss, shell_rs,
):
    gx = lax.axis_index("gx")
    gy = lax.axis_index("gy")
    n_gx = lax.axis_size("gx")
    n_gy = lax.axis_size("gy")
    up_y, down_y = lax.rem(gy + 1, n_gy), lax.rem(gy + n_gy - 1, n_gy)
    up_x, down_x = lax.rem(gx + 1, n_gx), lax.rem(gx + n_gx - 1, n_gx)

    barrier = pltpu.get_barrier_semaphore()

    def greet(k, carry):
        pl.semaphore_signal(barrier, inc=1, device_id=(gx, lax.rem(gy + k, n_gy)), device_id_type=MESH)
        return carry

    lax.fori_loop(1, n_gy, greet, 0)
    for other in (up_x, down_x):
        pl.semaphore_signal(barrier, inc=1, device_id=(other, gy), device_id_type=MESH)

    small = []
    for i, (src, dst) in enumerate(
        (
            (occ_hbm, occ_ref), (face_hbm, face_ref), (relay_hbm, relay_ref), (send_hbm, send_ref),
            (order_hbm, order_ref), (nbr_hbm, nbr_ref), (w_hbm, w_ref), (bias_hbm, bias_ref),
        )
    ):
        load = pltpu.make_async_copy(src, dst, small_sem.at[i])
        load.start()
        small.append(load)
    loads = []
    for g in range(4):
        load = pltpu.make_async_copy(feat_ref.at[pl.ds(8 * g, 8)], raw.at[pl.ds(8 * g, 8)], raw_sem.at[g])
        load.start()
        loads.append(load)

    small[0].wait()
    bits[...] = occupancy_bits(occ_ref[...].reshape(occ_ref.shape[0], HELD))
    rows = BS * BS
    own_row = jnp.where((iota((rows, LANES), 1) >> 3) == iota((rows, LANES), 0), 1.0, 0.0)
    spread = jnp.where((iota((LANES, LANES), 0) & 7) == (iota((LANES, LANES), 1) >> 6), 1.0, 0.0).astype(BF16)

    def mask_group(g, carry):
        picked = jnp.concatenate([bits[pl.ds(4 * g + i, 1), :] * own_row for i in range(4)], axis=0)
        wide = jnp.dot(picked.astype(BF16), spread, preferred_element_type=F32)
        wide = wide.reshape(4, BS, BS, LANES)
        mask[pl.ds(4 * g, 4)] = wide
        pool[pl.ds(4 * g, 4)] = raw[pl.ds(4 * g, 4)].astype(F32) * wide
        return carry

    for load in small[1:]:
        load.wait()
    build_bands(w_ref, inner_bands, (0, 1, 2, 3), True)
    for load in loads:
        load.wait()
    lax.fori_loop(0, HELD // 4, mask_group, 0)

    half = 2 * C
    lane = iota((BS, half), 1)
    row = iota((BS, half), 0)
    low_half = lane < C
    first_row = row == 0
    last_row = row == BS - 1
    edge_row = first_row | last_row

    def turn(v, by):
        return pltpu.roll(v, by % BS, axis=0)

    def between(parts):
        return [jnp.where(low_half, parts[q + 1], parts[q]) for q in range(3)]

    def joined(ends, middle):
        chain = [ends] + middle + [ends]
        return [jnp.where(low_half, chain[t], chain[t + 1]) for t in range(4)]

    def pack_shell(source, block, into, k):
        for side, x in enumerate((0, BS - 1)):
            for t in range(4):
                into[k, 4 * side + t] = source[block, x, :, t * half : (t + 1) * half].astype(BF16)
        strips = []
        for x in range(6):
            parts = [source[block, x + 1, :, t * half : (t + 1) * half] for t in range(4)]
            into[k, 8 + x] = jnp.where(low_half, parts[0], parts[3]).astype(BF16)
            strips += between(parts)
        for m in range(5):
            packed = strips[4 * m]
            for t, strip in enumerate(strips[4 * m + 1 : 4 * m + 4], 1):
                packed = jnp.where((row == 2 * t) | (row == 2 * t - 1), turn(strip, 2 * t), packed)
            into[k, 14 + m] = packed.astype(BF16)

    def outer_y(source, k):
        packed = [source[k, 14 + m].astype(F32) for m in range(5)]
        return [turn(packed[i // 4], -2 * (i % 4)) for i in range(18)]

    def unpack_shell(source, k, block, factor):
        for side, x in enumerate((0, BS - 1)):
            for t in range(4):
                pool[block, x, :, t * half : (t + 1) * half] = source[k, 4 * side + t].astype(F32) * factor
        strips = outer_y(source, k)
        for x in range(6):
            ends = source[k, 8 + x].astype(F32)
            for t, tile in enumerate(joined(ends, strips[3 * x : 3 * x + 3])):
                pool[block, x + 1, :, t * half : (t + 1) * half] = tile * factor

    def pick_faces(t, carry):
        pack_shell(pool, face_ref[0, t], fs_y, t)
        return carry

    lax.fori_loop(0, 2 * FACE, pick_faces, 0)
    pl.semaphore_wait(barrier, n_gy + 1)

    def exchange(src, dst, send, recv, up, down):
        copies = [
            pltpu.make_async_remote_copy(
                src_ref=src.at[pl.ds(FACE, FACE)], dst_ref=dst.at[pl.ds(0, FACE)],
                send_sem=send.at[0], recv_sem=recv.at[0], device_id=up, device_id_type=MESH),
            pltpu.make_async_remote_copy(
                src_ref=src.at[pl.ds(0, FACE)], dst_ref=dst.at[pl.ds(FACE, FACE)],
                send_sem=send.at[1], recv_sem=recv.at[1], device_id=down, device_id_type=MESH),
        ]
        for copy in copies:
            copy.start()
        return copies

    y_copies = exchange(fs_y, fr_y, ys, yr, (gx, up_y), (gx, down_y))
    pool[POOL - 1] = jnp.zeros((BS, BS, LANES), F32)

    my_x, my_z, my_core = gy // 8, lax.rem(gy // 2, 4), lax.rem(gy, 2)

    offsets = (
        ((2, 1), (2, 3), (1, 2), (3, 2)),
        ((1, 1), (3, 3), (1, 3), (3, 1)),
        ((1, 0), (3, 0), (0, 1), (0, 3)),
        ((2, 0), (0, 2), (2, 2), (0, 0)),
    )
    x_codes = [sum(offsets[g][i][0] * 4**g for g in range(4)) for i in range(4)]
    z_codes = [sum(offsets[g][i][1] * 4**g for g in range(4)) for i in range(4)]

    def peer(g, i, dc, sign):
        power = lax.shift_left(1, 2 * g)
        dx = lax.rem(x_codes[i] // power, 4)
        dz = lax.rem(z_codes[i] // power, 4)
        x = lax.rem(my_x + sign * dx + 4, 4)
        z = lax.rem(my_z + sign * dz + 4, 4)
        return 8 * x + 2 * z + lax.rem(my_core + dc, 2)

    bias = jnp.concatenate([bias_ref[...], bias_ref[...]], axis=1)

    def slot_of(g, i, dc):
        return jnp.maximum(send_ref[0, peer(g, i, dc, 1)], 0)

    def product(source, weight, planes, groups):
        sums = []
        for d in range(3):
            window = jnp.concatenate(
                [
                    jnp.concatenate(
                        [
                            source(d, j % 2, j // 2, lanes).reshape(planes * BATCH * BS, 2 * half)
                            for j in range(4)
                        ],
                        axis=1,
                    )
                    for lanes in groups
                ],
                axis=0,
            )
            part = jnp.dot(window, weight[d], preferred_element_type=F32)
            sums.append(part.reshape(len(groups) * planes * BATCH, BS, 4 * C))
        return sums[1] + pltpu.roll(sums[0], 1, axis=1) + pltpu.roll(sums[2], BS - 1, axis=1)

    def at_lanes(tile, count):
        return pl.ds(pl.multiple_of(half * tile, half), count * half)

    def mover(out, into, send, recv):
        def outgoing(g, i):
            k = BATCH * g + i
            return pltpu.make_async_remote_copy(
                src_ref=out.at[k], dst_ref=into.at[gy], send_sem=send.at[k], recv_sem=recv.at[k],
                device_id=(gx, peer(g, i // 2, i % 2, 1)), device_id_type=MESH)

        def incoming(g, i):
            k = BATCH * g + i
            source = peer(g, i // 2, i % 2, -1)
            return pltpu.make_async_remote_copy(
                src_ref=out.at[k], dst_ref=into.at[source], send_sem=send.at[k], recv_sem=recv.at[k],
                device_id=(gx, source), device_id_type=MESH)

        def each(g, act):
            for i in range(BATCH):
                if i == BATCH - 2:
                    pl.when(g < HELD // BATCH - 1)(lambda: act(g, BATCH - 2))
                else:
                    act(g, i)

        def start(g):
            each(g, lambda g, i: outgoing(g, i).start())

        def finish(g, carry):
            def wait(g, i):
                outgoing(g, i).wait_send()
                incoming(g, i).wait_recv()

            each(g, wait)
            return carry

        return start, finish

    def choose(g, carry):
        for i in range(BATCH):
            chosen[BATCH * g + i] = slot_of(g, i // 2, i % 2)
        return carry

    lax.fori_loop(0, HELD // BATCH, choose, 0)
    start_inner, finish_inner = mover(inner_out, inner_in, inner_ss, inner_rs)
    start_shell, finish_shell = mover(shell_out, shell_in, shell_ss, shell_rs)

    def inner_batch(g, carry):
        def gather(pair, inner):
            two = [chosen[BATCH * g + 2 * pair + dc] for dc in range(2)]
            for x in range(BS):
                both = jnp.concatenate([pool[two[0], x], pool[two[1], x]], axis=0)
                inner_tiles[x % 2, x // 2, pl.ds(pl.multiple_of(2 * BS * pair, 2 * BS), 2 * BS), :] = both.astype(BF16)
            return inner

        lax.fori_loop(0, BATCH // 2, gather, 0)
        slots = [chosen[BATCH * g + i] for i in range(BATCH)]

        total = product(
            lambda d, odd, first, lanes: inner_tiles[odd, first : first + 3, :, lanes],
            inner_bands, 3, [pl.ds(half * q, 2 * half) for q in range(3)])
        for b in range(BATCH):
            parts = []
            for x in range(6):
                keep = between([mask[slots[b], x + 1, :, t * half : (t + 1) * half] for t in range(4)])
                at = (x % 2) * half
                for q in range(3):
                    value = total[(3 * q + x // 2) * BATCH + b, :, at : at + half]
                    parts.append((value + bias) * keep[q])
            packed = []
            for m in range(4):
                for j in range(3):
                    packed.append(jnp.where(edge_row, turn(parts[4 * m + 3], 6 - 2 * j), parts[4 * m + j]))
            for m, part in enumerate(packed + parts[16:]):
                inner_out[BATCH * g + b, m] = part.astype(BF16)
        start_inner(g)
        return carry

    def block_rows(slot, ox, x):
        views = []
        for oy in range(3):
            around = [nbr_ref[9 * ox + 3 * oy + oz, 0, slot] for oz in range(3)]
            parts = [pool[around[0], x, :, 3 * half : 4 * half]]
            parts += [pool[around[1], x, :, t * half : (t + 1) * half] for t in range(4)]
            parts += [pool[around[2], x, :, 0:half]]
            views.append([jnp.where(low_half, parts[t + 1], parts[t]) for t in range(5)])
        before, here, after = views
        return (
            [jnp.where(last_row, b, h) for b, h in zip(before, here)],
            here,
            [jnp.where(first_row, a, h) for a, h in zip(after, here)],
        )

    def shell_batch(g, carry):
        def assemble(pair, inner):
            two = [chosen[BATCH * g + 2 * pair + dc] for dc in range(2)]
            for xx in range(BS + 2):
                ox = 0 if xx == 0 else (2 if xx == BS + 1 else 1)
                x = (xx - 1) % BS
                first, second = block_rows(two[0], ox, x), block_rows(two[1], ox, x)
                for d in range(3):
                    for t in range(5):
                        both = jnp.concatenate([first[d][t], second[d][t]], axis=0)
                        tiles[
                            d, xx % 2, xx // 2, pl.ds(pl.multiple_of(2 * BS * pair, 2 * BS), 2 * BS), t * half : (t + 1) * half
                        ] = both.astype(BF16)
            return inner

        lax.fori_loop(0, BATCH // 2, assemble, 0)
        slots = [chosen[BATCH * g + i] for i in range(BATCH)]

        def columns(step, inner):
            total = product(
                lambda d, odd, first, lanes: tiles[d, odd, first : first + 4, :, lanes],
                bands, 4, [at_lanes(GROUP * step + i, 2) for i in range(GROUP)])
            for i in range(GROUP):
                here = at_lanes(GROUP * step + i, 1)
                for b in range(BATCH):
                    for x in range(BS):
                        at = (x % 2) * half
                        part = total[(4 * i + x // 2) * BATCH + b, :, at : at + half] + bias
                        stage[b, x, :, here] = part * mask[slots[b], x, :, here]
            return inner

        lax.fori_loop(0, 4 // GROUP, columns, 0)

        def pack(b, inner):
            pack_shell(stage, b, shell_out, BATCH * g + b)
            return inner

        lax.fori_loop(0, BATCH, pack, 0)
        start_shell(g)
        return carry

    lax.fori_loop(0, EARLY, inner_batch, 0)
    for copy in y_copies:
        copy.wait_recv()
    low_y = jnp.where(gy > 0, 1.0, 0.0).astype(F32)
    high_y = jnp.where(gy < n_gy - 1, 1.0, 0.0).astype(F32)

    def take_y(t, carry):
        unpack_shell(fr_y, t, HELD + t, low_y)
        unpack_shell(fr_y, FACE + t, HELD + FACE + t, high_y)
        return carry

    lax.fori_loop(0, FACE, take_y, 0)

    def pick_relays(t, carry):
        pack_shell(pool, relay_ref[0, t], fs_x, t)
        return carry

    lax.fori_loop(0, 2 * FACE, pick_relays, 0)
    x_copies = exchange(fs_x, fr_x, xs, xr, (up_x, gy), (down_x, gy))
    lax.fori_loop(EARLY, HELD // BATCH, inner_batch, 0)
    build_bands(w_ref, bands, (1, 0, 3, 2), False)
    for copy in x_copies:
        copy.wait_recv()
    low_x = jnp.where(gx > 0, 1.0, 0.0).astype(F32)
    high_x = jnp.where(gx < n_gx - 1, 1.0, 0.0).astype(F32)

    def take_x(t, carry):
        unpack_shell(fr_x, t, HELD + 2 * FACE + t, low_x)
        unpack_shell(fr_x, FACE + t, HELD + 3 * FACE + t, high_x)
        return carry

    lax.fori_loop(0, FACE, take_x, 0)
    lax.fori_loop(0, HELD // BATCH, shell_batch, 0)
    inner_in[gy] = inner_out[HELD - 2]
    shell_in[gy] = shell_out[HELD - 2]
    for copy in y_copies + x_copies:
        copy.wait_send()
    lax.fori_loop(0, HELD // BATCH, finish_inner, 0)
    lax.fori_loop(0, HELD // BATCH, finish_shell, 0)

    def place(r, carry):
        source = order_ref[0, r]
        for side, x in enumerate((0, BS - 1)):
            for t in range(4):
                out_ref[r, x, :, t * half : (t + 1) * half] = shell_in[source, 4 * side + t]
        arrived = [inner_in[source, m].astype(F32) for m in range(INNER)]
        strips = outer_y(shell_in, source)
        middle = []
        for i in range(18):
            if i >= 16:
                tile = arrived[i - 4]
            elif i % 4 < 3:
                tile = arrived[3 * (i // 4) + i % 4]
            else:
                first, second, third = arrived[3 * (i // 4) : 3 * (i // 4) + 3]
                tile = jnp.where(row <= 2, turn(first, 2), jnp.where(row <= 4, turn(second, 4), turn(third, 6)))
            middle.append(jnp.where(edge_row, strips[i], tile))
        for x in range(6):
            ends = shell_in[source, 8 + x].astype(F32)
            for t, tile in enumerate(joined(ends, middle[3 * x : 3 * x + 3])):
                out_ref[r, x + 1, :, t * half : (t + 1) * half] = tile.astype(BF16)
        return carry

    lax.fori_loop(0, OUT, place, 0)


def on_device(features, occupancy, neighbors, face_lists, face_relays, send_slots, receive_order, weights, channel_bias):
    block = (BS, BS, LANES)
    out = pl.pallas_call(
        kernel,
        out_shape=jax.ShapeDtypeStruct((OUT,) + block, BF16),
        in_specs=[pl.BlockSpec(memory_space=pltpu.HBM)] * 9,
        out_specs=pl.BlockSpec(memory_space=pltpu.VMEM),
        scratch_shapes=[
            pltpu.SMEM((1, 2 * FACE), jnp.int32),
            pltpu.SMEM((1, 2 * FACE), jnp.int32),
            pltpu.SMEM((1, HELD), jnp.int32),
            pltpu.SMEM((1, OUT), jnp.int32),
            pltpu.SMEM((27, 1, HELD), jnp.int32),
            pltpu.VMEM((occupancy.shape[-1], 1, HELD), jnp.int32),
            pltpu.VMEM(weights.shape, BF16),
            pltpu.VMEM((1, C), F32),
            pltpu.SMEM((HELD,), jnp.int32),
            pltpu.VMEM((HELD,) + block, BF16),
            pltpu.VMEM((POOL,) + block, F32),
            pltpu.VMEM((HELD,) + block, F32),
            pltpu.VMEM((HELD, LANES), F32),
            pltpu.VMEM((2, 4, BATCH * BS, LANES), BF16),
            pltpu.VMEM((3, 16 * C, 4 * C), BF16),
            pltpu.VMEM((3, 2, 5, BATCH * BS, LANES + 2 * C), BF16),
            pltpu.VMEM((3, 16 * C, 4 * C), BF16),
            pltpu.VMEM((BATCH,) + block, F32),
            pltpu.VMEM((HELD, INNER, BS, 2 * C), BF16),
            pltpu.VMEM((HELD, INNER, BS, 2 * C), BF16),
            pltpu.VMEM((HELD, SHELL, BS, 2 * C), BF16),
            pltpu.VMEM((HELD, SHELL, BS, 2 * C), BF16),
            pltpu.VMEM((2 * FACE, SHELL, BS, 2 * C), BF16),
            pltpu.VMEM((2 * FACE, SHELL, BS, 2 * C), BF16),
            pltpu.VMEM((2 * FACE, SHELL, BS, 2 * C), BF16),
            pltpu.VMEM((2 * FACE, SHELL, BS, 2 * C), BF16),
            pltpu.SemaphoreType.DMA((8,)),
            pltpu.SemaphoreType.DMA((4,)),
            pltpu.SemaphoreType.DMA((2,)),
            pltpu.SemaphoreType.DMA((2,)),
            pltpu.SemaphoreType.DMA((2,)),
            pltpu.SemaphoreType.DMA((2,)),
            pltpu.SemaphoreType.DMA((HELD,)),
            pltpu.SemaphoreType.DMA((HELD,)),
            pltpu.SemaphoreType.DMA((HELD,)),
            pltpu.SemaphoreType.DMA((HELD,)),
        ],
        compiler_params=pltpu.CompilerParams(
            collective_id=0, has_side_effects=True, vmem_limit_bytes=50 << 20
        ),
    )(
        *(
            pltpu.with_memory_space_constraint(operand, pltpu.HBM)
            for operand in (
                face_lists[0],
                face_relays[0],
                send_slots[0, :, :, 0],
                receive_order[0],
                jnp.transpose(neighbors[0], (2, 0, 1)),
                jnp.transpose(occupancy[0], (2, 0, 1)),
                features[0, 0],
                weights,
                channel_bias.reshape(1, C),
            )
        )
    )
    return out[None, None]


def solution(mesh):
    in_specs = (
        P("gx", "gy", None, None, None, None),
        P("gx", "gy", None, None),
        P("gx", "gy", None, None),
        P("gx", "gy", None),
        P("gx", "gy", None),
        P("gx", "gy", None, None),
        P("gx", "gy", None),
        P(),
        P(),
    )
    out_specs = P("gx", "gy", None, None, None, None)
    return jax.shard_map(
        on_device, mesh=mesh, in_specs=in_specs, out_specs=out_specs, check_vma=False
    )
```

```python
import jax
import jax.numpy as jnp
from jax import lax
from jax.experimental import pallas as pl
from jax.experimental.pallas import tpu as pltpu
from jax.sharding import PartitionSpec as P

C = 64
BS = 8
LANES = BS * C
HELD = 32
FACE = 4
OUT = 16
POOL = 49
BATCH = 4
EARLY = 2
GROUP = 4
INNER = 14
SHELL = 19
WORD_BITS = 21
MESH = pl.DeviceIdType.MESH
F32 = jnp.float32
BF16 = jnp.bfloat16


def iota(shape, dim):
    return lax.broadcasted_iota(jnp.int32, shape, dim)


def occupancy_bits(words):
    width, slots = words.shape
    voxels = BS**3
    chunks = jnp.concatenate([words & 127, (words >> 7) & 127, words >> 14], axis=1)
    voxel = iota((width, voxels), 1)
    pick = ((voxel * 3121) >> 16) == iota((width, voxels), 0)
    picked = lax.dot_general(
        chunks.astype(F32).astype(BF16),
        jnp.where(pick, 1.0, 0.0).astype(BF16),
        (((0,), (0,)), ((), ())),
        preferred_element_type=F32,
    ).astype(jnp.int32)
    v = iota((slots, voxels), 1)
    bit = v - WORD_BITS * ((v * 3121) >> 16)
    low, mid, high = picked[:slots], picked[slots : 2 * slots], picked[2 * slots :]
    chunk = jnp.where(bit < 7, low, jnp.where(bit < 14, mid, high))
    shift = bit - jnp.where(bit >= 7, 7, 0) - jnp.where(bit >= 14, 7, 0)
    return ((chunk >> shift) & 1).astype(F32)


def build_bands(w_ref, bands, z_order, swapped):
    zero = jnp.zeros((C, C), BF16)
    for d in range(3):
        for a in range(3):
            taps = [w_ref[9 * a + 3 * d + c] for c in range(3)]
            for k, rz in enumerate(z_order):
                ends = [taps[rz] if rz <= 2 else zero, taps[rz - 1] if rz >= 1 else zero]
                pair = jnp.concatenate(ends[::-1] if swapped else ends, axis=1)
                for xo in range(2):
                    bands[d, pl.ds((a + xo) * 4 * C + k * C, C), xo * 2 * C : (xo + 1) * 2 * C] = pair
        blank = jnp.zeros((4 * C, 2 * C), BF16)
        bands[d, 0 : 4 * C, 2 * C : 4 * C] = blank
        bands[d, 12 * C : 16 * C, 0 : 2 * C] = blank


def kernel(
    face_hbm, relay_hbm, send_hbm, order_hbm, nbr_hbm, occ_hbm, feat_ref, w_hbm, bias_hbm,
    out_ref,
    face_ref, relay_ref, send_ref, order_ref, nbr_ref, occ_ref, w_ref, bias_ref, chosen, raw, pool, mask, bits,
    inner_tiles, inner_bands, tiles, bands, stage, inner_out, inner_in, shell_out, shell_in,
    fs_y, fr_y, fs_x, fr_x,
    small_sem, raw_sem, ys, yr, xs, xr, inner_ss, inner_rs, shell_ss, shell_rs,
):
    gx = lax.axis_index("gx")
    gy = lax.axis_index("gy")
    n_gx = lax.axis_size("gx")
    n_gy = lax.axis_size("gy")
    up_y, down_y = lax.rem(gy + 1, n_gy), lax.rem(gy + n_gy - 1, n_gy)
    up_x, down_x = lax.rem(gx + 1, n_gx), lax.rem(gx + n_gx - 1, n_gx)

    barrier = pltpu.get_barrier_semaphore()

    def greet(k, carry):
        pl.semaphore_signal(barrier, inc=1, device_id=(gx, lax.rem(gy + k, n_gy)), device_id_type=MESH)
        return carry

    lax.fori_loop(1, n_gy, greet, 0)
    for other in (up_x, down_x):
        pl.semaphore_signal(barrier, inc=1, device_id=(other, gy), device_id_type=MESH)

    small = []
    for i, (src, dst) in enumerate(
        (
            (occ_hbm, occ_ref), (face_hbm, face_ref), (relay_hbm, relay_ref), (send_hbm, send_ref),
            (order_hbm, order_ref), (nbr_hbm, nbr_ref), (w_hbm, w_ref), (bias_hbm, bias_ref),
        )
    ):
        load = pltpu.make_async_copy(src, dst, small_sem.at[i])
        load.start()
        small.append(load)
    loads = []
    for g in range(4):
        load = pltpu.make_async_copy(feat_ref.at[pl.ds(8 * g, 8)], raw.at[pl.ds(8 * g, 8)], raw_sem.at[g])
        load.start()
        loads.append(load)

    small[0].wait()
    bits[...] = occupancy_bits(occ_ref[...].reshape(occ_ref.shape[0], HELD))
    rows = BS * BS
    own_row = jnp.where((iota((rows, LANES), 1) >> 3) == iota((rows, LANES), 0), 1.0, 0.0)
    spread = jnp.where((iota((LANES, LANES), 0) & 7) == (iota((LANES, LANES), 1) >> 6), 1.0, 0.0).astype(BF16)

    def mask_group(g, carry):
        picked = jnp.concatenate([bits[pl.ds(4 * g + i, 1), :] * own_row for i in range(4)], axis=0)
        wide = jnp.dot(picked.astype(BF16), spread, preferred_element_type=F32)
        wide = wide.reshape(4, BS, BS, LANES)
        mask[pl.ds(4 * g, 4)] = wide
        pool[pl.ds(4 * g, 4)] = raw[pl.ds(4 * g, 4)].astype(F32) * wide
        return carry

    for load in small[1:]:
        load.wait()
    build_bands(w_ref, inner_bands, (0, 1, 2, 3), True)
    for load in loads:
        load.wait()
    lax.fori_loop(0, HELD // 4, mask_group, 0)

    half = 2 * C
    lane = iota((BS, half), 1)
    row = iota((BS, half), 0)
    low_half = lane < C
    first_row = row == 0
    last_row = row == BS - 1
    edge_row = first_row | last_row

    def turn(v, by):
        return pltpu.roll(v, by % BS, axis=0)

    def between(parts):
        return [jnp.where(low_half, parts[q + 1], parts[q]) for q in range(3)]

    def joined(ends, middle):
        chain = [ends] + middle + [ends]
        return [jnp.where(low_half, chain[t], chain[t + 1]) for t in range(4)]

    def pack_shell(source, block, into, k):
        for side, x in enumerate((0, BS - 1)):
            for t in range(4):
                into[k, 4 * side + t] = source[block, x, :, t * half : (t + 1) * half].astype(BF16)
        strips = []
        for x in range(6):
            parts = [source[block, x + 1, :, t * half : (t + 1) * half] for t in range(4)]
            into[k, 8 + x] = jnp.where(low_half, parts[0], parts[3]).astype(BF16)
            strips += between(parts)
        for m in range(5):
            packed = strips[4 * m]
            for t, strip in enumerate(strips[4 * m + 1 : 4 * m + 4], 1):
                packed = jnp.where((row == 2 * t) | (row == 2 * t - 1), turn(strip, 2 * t), packed)
            into[k, 14 + m] = packed.astype(BF16)

    def outer_y(source, k):
        packed = [source[k, 14 + m].astype(F32) for m in range(5)]
        return [turn(packed[i // 4], -2 * (i % 4)) for i in range(18)]

    def unpack_shell(source, k, block, factor):
        for side, x in enumerate((0, BS - 1)):
            for t in range(4):
                pool[block, x, :, t * half : (t + 1) * half] = source[k, 4 * side + t].astype(F32) * factor
        strips = outer_y(source, k)
        for x in range(6):
            ends = source[k, 8 + x].astype(F32)
            for t, tile in enumerate(joined(ends, strips[3 * x : 3 * x + 3])):
                pool[block, x + 1, :, t * half : (t + 1) * half] = tile * factor

    pl.semaphore_wait(barrier, n_gy + 1)

    def exchange(out, into, send, recv, up, down, index, first, low, high):
        def copy(t, device):
            slot = lax.rem(t + FACE, 2 * FACE)
            return pltpu.make_async_remote_copy(
                src_ref=out.at[t], dst_ref=into.at[slot], send_sem=send.at[t], recv_sem=recv.at[slot],
                device_id=device, device_id_type=MESH)

        def pick(t, carry):
            pack_shell(pool, index[0, t], out, t)
            copy(t, down).start()
            pack_shell(pool, index[0, FACE + t], out, FACE + t)
            copy(FACE + t, up).start()
            return carry

        def take(t, carry):
            copy(FACE + t, up).wait_recv()
            unpack_shell(into, t, first + t, low)
            copy(t, down).wait_recv()
            unpack_shell(into, FACE + t, first + FACE + t, high)
            return carry

        def settle(t, carry):
            copy(t, down).wait_send()
            copy(FACE + t, up).wait_send()
            return carry

        return [lambda act=act: lax.fori_loop(0, FACE, act, 0) for act in (pick, take, settle)]

    def inside(condition):
        return jnp.where(condition, 1.0, 0.0).astype(F32)

    send_y, take_y, settle_y = exchange(
        fs_y, fr_y, ys, yr, (gx, up_y), (gx, down_y), face_ref, HELD, inside(gy > 0), inside(gy < n_gy - 1))
    send_x, take_x, settle_x = exchange(
        fs_x, fr_x, xs, xr, (up_x, gy), (down_x, gy), relay_ref, HELD + 2 * FACE,
        inside(gx > 0), inside(gx < n_gx - 1))
    send_y()
    pool[POOL - 1] = jnp.zeros((BS, BS, LANES), F32)

    my_x, my_z, my_core = gy // 8, lax.rem(gy // 2, 4), lax.rem(gy, 2)

    offsets = (
        ((2, 1), (1, 2)), ((2, 3), (3, 2)), ((1, 1), (3, 3)), ((1, 3), (3, 1)),
        ((1, 0), (3, 0)), ((0, 1), (0, 3)), ((2, 0), (0, 2)), ((2, 2), (0, 0)),
    )
    x_codes = [sum(pair[i][0] * 4**g for g, pair in enumerate(offsets)) for i in range(2)]
    z_codes = [sum(pair[i][1] * 4**g for g, pair in enumerate(offsets)) for i in range(2)]

    def peer(g, i, dc, sign):
        power = lax.shift_left(1, 2 * g)
        dx = lax.rem(x_codes[i] // power, 4)
        dz = lax.rem(z_codes[i] // power, 4)
        x = lax.rem(my_x + sign * dx + 4, 4)
        z = lax.rem(my_z + sign * dz + 4, 4)
        return 8 * x + 2 * z + lax.rem(my_core + dc, 2)

    bias = jnp.concatenate([bias_ref[...], bias_ref[...]], axis=1)

    def slot_of(g, i, dc):
        return jnp.maximum(send_ref[0, peer(g, i, dc, 1)], 0)

    def product(source, weight, planes, groups):
        sums = []
        for d in range(3):
            window = jnp.concatenate(
                [
                    jnp.concatenate(
                        [
                            source(d, j % 2, j // 2, lanes).reshape(planes * BATCH * BS, 2 * half)
                            for j in range(4)
                        ],
                        axis=1,
                    )
                    for lanes in groups
                ],
                axis=0,
            )
            part = jnp.dot(window, weight[d], preferred_element_type=F32)
            sums.append(part.reshape(len(groups) * planes * BATCH, BS, 4 * C))
        return sums[1] + pltpu.roll(sums[0], 1, axis=1) + pltpu.roll(sums[2], BS - 1, axis=1)

    def at_lanes(tile, count):
        return pl.ds(pl.multiple_of(half * tile, half), count * half)

    def mover(out, into, send, recv):
        def outgoing(g, i):
            k = BATCH * g + i
            return pltpu.make_async_remote_copy(
                src_ref=out.at[k], dst_ref=into.at[gy], send_sem=send.at[k], recv_sem=recv.at[k],
                device_id=(gx, peer(g, i // 2, i % 2, 1)), device_id_type=MESH)

        def incoming(g, i):
            k = BATCH * g + i
            source = peer(g, i // 2, i % 2, -1)
            return pltpu.make_async_remote_copy(
                src_ref=out.at[k], dst_ref=into.at[source], send_sem=send.at[k], recv_sem=recv.at[k],
                device_id=(gx, source), device_id_type=MESH)

        def each(g, act):
            for i in range(BATCH):
                if i == BATCH - 2:
                    pl.when(g < HELD // BATCH - 1)(lambda: act(g, BATCH - 2))
                else:
                    act(g, i)

        def start(g):
            each(g, lambda g, i: outgoing(g, i).start())

        def finish(g, carry):
            def wait(g, i):
                outgoing(g, i).wait_send()
                incoming(g, i).wait_recv()

            each(g, wait)
            return carry

        return start, finish

    def choose(g, carry):
        for i in range(BATCH):
            chosen[BATCH * g + i] = slot_of(g, i // 2, i % 2)
        return carry

    lax.fori_loop(0, HELD // BATCH, choose, 0)
    start_inner, finish_inner = mover(inner_out, inner_in, inner_ss, inner_rs)
    start_shell, finish_shell = mover(shell_out, shell_in, shell_ss, shell_rs)

    def inner_batch(g, carry):
        def gather(pair, inner):
            two = [chosen[BATCH * g + 2 * pair + dc] for dc in range(2)]
            for x in range(BS):
                both = jnp.concatenate([pool[two[0], x], pool[two[1], x]], axis=0)
                inner_tiles[x % 2, x // 2, pl.ds(pl.multiple_of(2 * BS * pair, 2 * BS), 2 * BS), :] = both.astype(BF16)
            return inner

        lax.fori_loop(0, BATCH // 2, gather, 0)
        slots = [chosen[BATCH * g + i] for i in range(BATCH)]

        total = product(
            lambda d, odd, first, lanes: inner_tiles[odd, first : first + 3, :, lanes],
            inner_bands, 3, [pl.ds(half * q, 2 * half) for q in range(3)])
        for b in range(BATCH):
            parts = []
            for x in range(6):
                keep = between([mask[slots[b], x + 1, :, t * half : (t + 1) * half] for t in range(4)])
                at = (x % 2) * half
                for q in range(3):
                    value = total[(3 * q + x // 2) * BATCH + b, :, at : at + half]
                    parts.append((value + bias) * keep[q])
            packed = []
            for m in range(4):
                for j in range(3):
                    packed.append(jnp.where(edge_row, turn(parts[4 * m + 3], 6 - 2 * j), parts[4 * m + j]))
            for m, part in enumerate(packed + parts[16:]):
                inner_out[BATCH * g + b, m] = part.astype(BF16)
        start_inner(g)
        return carry

    def block_rows(slot, ox, x):
        views = []
        for oy in range(3):
            around = [nbr_ref[9 * ox + 3 * oy + oz, 0, slot] for oz in range(3)]
            parts = [pool[around[0], x, :, 3 * half : 4 * half]]
            parts += [pool[around[1], x, :, t * half : (t + 1) * half] for t in range(4)]
            parts += [pool[around[2], x, :, 0:half]]
            views.append([jnp.where(low_half, parts[t + 1], parts[t]) for t in range(5)])
        before, here, after = views
        return (
            [jnp.where(last_row, b, h) for b, h in zip(before, here)],
            here,
            [jnp.where(first_row, a, h) for a, h in zip(after, here)],
        )

    def shell_batch(g, carry):
        def assemble(pair, inner):
            two = [chosen[BATCH * g + 2 * pair + dc] for dc in range(2)]
            for xx in range(BS + 2):
                ox = 0 if xx == 0 else (2 if xx == BS + 1 else 1)
                x = (xx - 1) % BS
                first, second = block_rows(two[0], ox, x), block_rows(two[1], ox, x)
                for d in range(3):
                    for t in range(5):
                        both = jnp.concatenate([first[d][t], second[d][t]], axis=0)
                        tiles[
                            d, xx % 2, xx // 2, pl.ds(pl.multiple_of(2 * BS * pair, 2 * BS), 2 * BS), t * half : (t + 1) * half
                        ] = both.astype(BF16)
            return inner

        lax.fori_loop(0, BATCH // 2, assemble, 0)
        slots = [chosen[BATCH * g + i] for i in range(BATCH)]

        def columns(step, inner):
            total = product(
                lambda d, odd, first, lanes: tiles[d, odd, first : first + 4, :, lanes],
                bands, 4, [at_lanes(GROUP * step + i, 2) for i in range(GROUP)])
            for i in range(GROUP):
                here = at_lanes(GROUP * step + i, 1)
                for b in range(BATCH):
                    for x in range(BS):
                        at = (x % 2) * half
                        part = total[(4 * i + x // 2) * BATCH + b, :, at : at + half] + bias
                        stage[b, x, :, here] = part * mask[slots[b], x, :, here]
            return inner

        lax.fori_loop(0, 4 // GROUP, columns, 0)

        def pack(b, inner):
            pack_shell(stage, b, shell_out, BATCH * g + b)
            return inner

        lax.fori_loop(0, BATCH, pack, 0)
        start_shell(g)
        return carry

    lax.fori_loop(0, EARLY, inner_batch, 0)
    take_y()
    send_x()
    lax.fori_loop(EARLY, HELD // BATCH, inner_batch, 0)
    build_bands(w_ref, bands, (1, 0, 3, 2), False)
    take_x()
    lax.fori_loop(0, HELD // BATCH, shell_batch, 0)
    inner_in[gy] = inner_out[HELD - 2]
    shell_in[gy] = shell_out[HELD - 2]
    settle_y()
    settle_x()
    lax.fori_loop(0, HELD // BATCH, finish_inner, 0)
    lax.fori_loop(0, HELD // BATCH, finish_shell, 0)

    def place(r, carry):
        source = order_ref[0, r]
        for side, x in enumerate((0, BS - 1)):
            for t in range(4):
                out_ref[r, x, :, t * half : (t + 1) * half] = shell_in[source, 4 * side + t]
        arrived = [inner_in[source, m].astype(F32) for m in range(INNER)]
        strips = outer_y(shell_in, source)
        middle = []
        for i in range(18):
            if i >= 16:
                tile = arrived[i - 4]
            elif i % 4 < 3:
                tile = arrived[3 * (i // 4) + i % 4]
            else:
                first, second, third = arrived[3 * (i // 4) : 3 * (i // 4) + 3]
                tile = jnp.where(row <= 2, turn(first, 2), jnp.where(row <= 4, turn(second, 4), turn(third, 6)))
            middle.append(jnp.where(edge_row, strips[i], tile))
        for x in range(6):
            ends = shell_in[source, 8 + x].astype(F32)
            for t, tile in enumerate(joined(ends, middle[3 * x : 3 * x + 3])):
                out_ref[r, x + 1, :, t * half : (t + 1) * half] = tile.astype(BF16)
        return carry

    lax.fori_loop(0, OUT, place, 0)


def on_device(features, occupancy, neighbors, face_lists, face_relays, send_slots, receive_order, weights, channel_bias):
    block = (BS, BS, LANES)
    out = pl.pallas_call(
        kernel,
        out_shape=jax.ShapeDtypeStruct((OUT,) + block, BF16),
        in_specs=[pl.BlockSpec(memory_space=pltpu.HBM)] * 9,
        out_specs=pl.BlockSpec(memory_space=pltpu.VMEM),
        scratch_shapes=[
            pltpu.SMEM((1, 2 * FACE), jnp.int32),
            pltpu.SMEM((1, 2 * FACE), jnp.int32),
            pltpu.SMEM((1, HELD), jnp.int32),
            pltpu.SMEM((1, OUT), jnp.int32),
            pltpu.SMEM((27, 1, HELD), jnp.int32),
            pltpu.VMEM((occupancy.shape[-1], 1, HELD), jnp.int32),
            pltpu.VMEM(weights.shape, BF16),
            pltpu.VMEM((1, C), F32),
            pltpu.SMEM((HELD,), jnp.int32),
            pltpu.VMEM((HELD,) + block, BF16),
            pltpu.VMEM((POOL,) + block, F32),
            pltpu.VMEM((HELD,) + block, F32),
            pltpu.VMEM((HELD, LANES), F32),
            pltpu.VMEM((2, 4, BATCH * BS, LANES), BF16),
            pltpu.VMEM((3, 16 * C, 4 * C), BF16),
            pltpu.VMEM((3, 2, 5, BATCH * BS, LANES + 2 * C), BF16),
            pltpu.VMEM((3, 16 * C, 4 * C), BF16),
            pltpu.VMEM((BATCH,) + block, F32),
            pltpu.VMEM((HELD, INNER, BS, 2 * C), BF16),
            pltpu.VMEM((HELD, INNER, BS, 2 * C), BF16),
            pltpu.VMEM((HELD, SHELL, BS, 2 * C), BF16),
            pltpu.VMEM((HELD, SHELL, BS, 2 * C), BF16),
            pltpu.VMEM((2 * FACE, SHELL, BS, 2 * C), BF16),
            pltpu.VMEM((2 * FACE, SHELL, BS, 2 * C), BF16),
            pltpu.VMEM((2 * FACE, SHELL, BS, 2 * C), BF16),
            pltpu.VMEM((2 * FACE, SHELL, BS, 2 * C), BF16),
            pltpu.SemaphoreType.DMA((8,)),
            pltpu.SemaphoreType.DMA((4,)),
            pltpu.SemaphoreType.DMA((2 * FACE,)),
            pltpu.SemaphoreType.DMA((2 * FACE,)),
            pltpu.SemaphoreType.DMA((2 * FACE,)),
            pltpu.SemaphoreType.DMA((2 * FACE,)),
            pltpu.SemaphoreType.DMA((HELD,)),
            pltpu.SemaphoreType.DMA((HELD,)),
            pltpu.SemaphoreType.DMA((HELD,)),
            pltpu.SemaphoreType.DMA((HELD,)),
        ],
        compiler_params=pltpu.CompilerParams(
            collective_id=0, has_side_effects=True, vmem_limit_bytes=50 << 20
        ),
    )(
        *(
            pltpu.with_memory_space_constraint(operand, pltpu.HBM)
            for operand in (
                face_lists[0],
                face_relays[0],
                send_slots[0, :, :, 0],
                receive_order[0],
                jnp.transpose(neighbors[0], (2, 0, 1)),
                jnp.transpose(occupancy[0], (2, 0, 1)),
                features[0, 0],
                weights,
                channel_bias.reshape(1, C),
            )
        )
    )
    return out[None, None]


def solution(mesh):
    in_specs = (
        P("gx", "gy", None, None, None, None),
        P("gx", "gy", None, None),
        P("gx", "gy", None, None),
        P("gx", "gy", None),
        P("gx", "gy", None),
        P("gx", "gy", None, None),
        P("gx", "gy", None),
        P(),
        P(),
    )
    out_specs = P("gx", "gy", None, None, None, None)
    return jax.shard_map(
        on_device, mesh=mesh, in_specs=in_specs, out_specs=out_specs, check_vma=False
    )
```

```python
import jax
import jax.numpy as jnp
from jax import lax
from jax.experimental import pallas as pl
from jax.experimental.pallas import tpu as pltpu
from jax.sharding import PartitionSpec as P

C = 64
BS = 8
LANES = BS * C
HELD = 32
FACE = 4
OUT = 16
POOL = 49
BATCH = 4
EARLY = 2
GROUP = 4
INNER = 14
SHELL = 19
WORD_BITS = 21
MESH = pl.DeviceIdType.MESH
F32 = jnp.float32
BF16 = jnp.bfloat16


def iota(shape, dim):
    return lax.broadcasted_iota(jnp.int32, shape, dim)


def occupancy_bits(words):
    width, slots = words.shape
    voxels = BS**3
    chunks = jnp.concatenate([words & 127, (words >> 7) & 127, words >> 14], axis=1)
    voxel = iota((width, voxels), 1)
    pick = ((voxel * 3121) >> 16) == iota((width, voxels), 0)
    picked = lax.dot_general(
        chunks.astype(F32).astype(BF16),
        jnp.where(pick, 1.0, 0.0).astype(BF16),
        (((0,), (0,)), ((), ())),
        preferred_element_type=F32,
    ).astype(jnp.int32)
    v = iota((slots, voxels), 1)
    bit = v - WORD_BITS * ((v * 3121) >> 16)
    low, mid, high = picked[:slots], picked[slots : 2 * slots], picked[2 * slots :]
    chunk = jnp.where(bit < 7, low, jnp.where(bit < 14, mid, high))
    shift = bit - jnp.where(bit >= 7, 7, 0) - jnp.where(bit >= 14, 7, 0)
    return ((chunk >> shift) & 1).astype(F32)


def build_bands(w_ref, bands, z_order, swapped):
    zero = jnp.zeros((C, C), BF16)
    for d in range(3):
        for a in range(3):
            taps = [w_ref[9 * a + 3 * d + c] for c in range(3)]
            for k, rz in enumerate(z_order):
                ends = [taps[rz] if rz <= 2 else zero, taps[rz - 1] if rz >= 1 else zero]
                pair = jnp.concatenate(ends[::-1] if swapped else ends, axis=1)
                for xo in range(2):
                    bands[d, pl.ds((a + xo) * 4 * C + k * C, C), xo * 2 * C : (xo + 1) * 2 * C] = pair
        blank = jnp.zeros((4 * C, 2 * C), BF16)
        bands[d, 0 : 4 * C, 2 * C : 4 * C] = blank
        bands[d, 12 * C : 16 * C, 0 : 2 * C] = blank


def kernel(
    face_hbm, relay_hbm, send_hbm, order_hbm, nbr_hbm, occ_hbm, feat_ref, w_hbm, bias_hbm,
    out_ref,
    face_ref, relay_ref, send_ref, order_ref, nbr_ref, occ_ref, w_ref, bias_ref, chosen, raw, pool, mask, bits,
    inner_tiles, inner_bands, tiles, bands, stage, inner_out, inner_in, shell_out, shell_in,
    fs_y, fr_y, fs_x, fr_x,
    small_sem, raw_sem, ys, yr, xs, xr, inner_ss, inner_rs, shell_ss, shell_rs,
):
    gx = lax.axis_index("gx")
    gy = lax.axis_index("gy")
    n_gx = lax.axis_size("gx")
    n_gy = lax.axis_size("gy")
    up_y, down_y = lax.rem(gy + 1, n_gy), lax.rem(gy + n_gy - 1, n_gy)
    up_x, down_x = lax.rem(gx + 1, n_gx), lax.rem(gx + n_gx - 1, n_gx)

    barrier = pltpu.get_barrier_semaphore()

    def greet(k, carry):
        pl.semaphore_signal(barrier, inc=1, device_id=(gx, lax.rem(gy + k, n_gy)), device_id_type=MESH)
        return carry

    lax.fori_loop(1, n_gy, greet, 0)
    for other in (up_x, down_x):
        pl.semaphore_signal(barrier, inc=1, device_id=(other, gy), device_id_type=MESH)

    small = []
    for i, (src, dst) in enumerate(
        (
            (occ_hbm, occ_ref), (face_hbm, face_ref), (relay_hbm, relay_ref), (send_hbm, send_ref),
            (order_hbm, order_ref), (nbr_hbm, nbr_ref), (w_hbm, w_ref), (bias_hbm, bias_ref),
        )
    ):
        load = pltpu.make_async_copy(src, dst, small_sem.at[i])
        load.start()
        small.append(load)
    loads = []
    for g in range(4):
        load = pltpu.make_async_copy(feat_ref.at[pl.ds(8 * g, 8)], raw.at[pl.ds(8 * g, 8)], raw_sem.at[g])
        load.start()
        loads.append(load)

    small[0].wait()
    bits[...] = occupancy_bits(occ_ref[...].reshape(occ_ref.shape[0], HELD))
    rows = BS * BS
    own_row = jnp.where((iota((rows, LANES), 1) >> 3) == iota((rows, LANES), 0), 1.0, 0.0)
    spread = jnp.where((iota((LANES, LANES), 0) & 7) == (iota((LANES, LANES), 1) >> 6), 1.0, 0.0).astype(BF16)

    def mask_group(g, carry):
        picked = jnp.concatenate([bits[pl.ds(4 * g + i, 1), :] * own_row for i in range(4)], axis=0)
        wide = jnp.dot(picked.astype(BF16), spread, preferred_element_type=F32)
        wide = wide.reshape(4, BS, BS, LANES)
        mask[pl.ds(4 * g, 4)] = wide
        pool[pl.ds(4 * g, 4)] = raw[pl.ds(4 * g, 4)].astype(F32) * wide
        return carry

    for load in small[1:]:
        load.wait()
    build_bands(w_ref, inner_bands, (0, 1, 2, 3), True)
    for g, load in enumerate(loads):
        load.wait()
        lax.fori_loop(2 * g, 2 * g + 2, mask_group, 0)

    half = 2 * C
    lane = iota((BS, half), 1)
    row = iota((BS, half), 0)
    low_half = lane < C
    first_row = row == 0
    last_row = row == BS - 1
    edge_row = first_row | last_row

    def turn(v, by):
        return pltpu.roll(v, by % BS, axis=0)

    def between(parts):
        return [jnp.where(low_half, parts[q + 1], parts[q]) for q in range(3)]

    def joined(ends, middle):
        chain = [ends] + middle + [ends]
        return [jnp.where(low_half, chain[t], chain[t + 1]) for t in range(4)]

    def pack_shell(source, block, into, k):
        for side, x in enumerate((0, BS - 1)):
            for t in range(4):
                into[k, 4 * side + t] = source[block, x, :, t * half : (t + 1) * half].astype(BF16)
        strips = []
        for x in range(6):
            parts = [source[block, x + 1, :, t * half : (t + 1) * half] for t in range(4)]
            into[k, 8 + x] = jnp.where(low_half, parts[0], parts[3]).astype(BF16)
            strips += between(parts)
        for m in range(5):
            packed = strips[4 * m]
            for t, strip in enumerate(strips[4 * m + 1 : 4 * m + 4], 1):
                packed = jnp.where((row == 2 * t) | (row == 2 * t - 1), turn(strip, 2 * t), packed)
            into[k, 14 + m] = packed.astype(BF16)

    def outer_y(source, k):
        packed = [source[k, 14 + m].astype(F32) for m in range(5)]
        return [turn(packed[i // 4], -2 * (i % 4)) for i in range(18)]

    def unpack_shell(source, k, block, factor):
        for side, x in enumerate((0, BS - 1)):
            for t in range(4):
                pool[block, x, :, t * half : (t + 1) * half] = source[k, 4 * side + t].astype(F32) * factor
        strips = outer_y(source, k)
        for x in range(6):
            ends = source[k, 8 + x].astype(F32)
            for t, tile in enumerate(joined(ends, strips[3 * x : 3 * x + 3])):
                pool[block, x + 1, :, t * half : (t + 1) * half] = tile * factor

    pl.semaphore_wait(barrier, n_gy + 1)

    def exchange(out, into, send, recv, up, down, index, first, low, high):
        def copy(t, device):
            slot = lax.rem(t + FACE, 2 * FACE)
            return pltpu.make_async_remote_copy(
                src_ref=out.at[t], dst_ref=into.at[slot], send_sem=send.at[t], recv_sem=recv.at[slot],
                device_id=device, device_id_type=MESH)

        def pick(t, carry):
            pack_shell(pool, index[0, t], out, t)
            copy(t, down).start()
            pack_shell(pool, index[0, FACE + t], out, FACE + t)
            copy(FACE + t, up).start()
            return carry

        def take(t, carry):
            copy(FACE + t, up).wait_recv()
            unpack_shell(into, t, first + t, low)
            copy(t, down).wait_recv()
            unpack_shell(into, FACE + t, first + FACE + t, high)
            return carry

        def settle(t, carry):
            copy(t, down).wait_send()
            copy(FACE + t, up).wait_send()
            return carry

        return [lambda act=act: lax.fori_loop(0, FACE, act, 0) for act in (pick, take, settle)]

    def inside(condition):
        return jnp.where(condition, 1.0, 0.0).astype(F32)

    send_y, take_y, settle_y = exchange(
        fs_y, fr_y, ys, yr, (gx, up_y), (gx, down_y), face_ref, HELD, inside(gy > 0), inside(gy < n_gy - 1))
    send_x, take_x, settle_x = exchange(
        fs_x, fr_x, xs, xr, (up_x, gy), (down_x, gy), relay_ref, HELD + 2 * FACE,
        inside(gx > 0), inside(gx < n_gx - 1))
    send_y()
    pool[POOL - 1] = jnp.zeros((BS, BS, LANES), F32)

    my_x, my_z, my_core = gy // 8, lax.rem(gy // 2, 4), lax.rem(gy, 2)

    offsets = (
        ((2, 1), (1, 2)), ((2, 3), (3, 2)), ((2, 0), (0, 2)), ((1, 1), (3, 3)),
        ((1, 3), (3, 1)), ((2, 2), (1, 0)), ((3, 0), (0, 1)), ((0, 3), (0, 0)),
    )
    x_codes = [sum(pair[i][0] * 4**g for g, pair in enumerate(offsets)) for i in range(2)]
    z_codes = [sum(pair[i][1] * 4**g for g, pair in enumerate(offsets)) for i in range(2)]

    def peer(g, i, dc, sign):
        power = lax.shift_left(1, 2 * g)
        dx = lax.rem(x_codes[i] // power, 4)
        dz = lax.rem(z_codes[i] // power, 4)
        x = lax.rem(my_x + sign * dx + 4, 4)
        z = lax.rem(my_z + sign * dz + 4, 4)
        return 8 * x + 2 * z + lax.rem(my_core + dc, 2)

    bias = jnp.concatenate([bias_ref[...], bias_ref[...]], axis=1)

    def slot_of(g, i, dc):
        return jnp.maximum(send_ref[0, peer(g, i, dc, 1)], 0)

    def product(source, weight, planes, groups):
        sums = []
        for d in range(3):
            window = jnp.concatenate(
                [
                    jnp.concatenate(
                        [
                            source(d, j % 2, j // 2, lanes).reshape(planes * BATCH * BS, 2 * half)
                            for j in range(4)
                        ],
                        axis=1,
                    )
                    for lanes in groups
                ],
                axis=0,
            )
            part = jnp.dot(window, weight[d], preferred_element_type=F32)
            sums.append(part.reshape(len(groups) * planes * BATCH, BS, 4 * C))
        return sums[1] + pltpu.roll(sums[0], 1, axis=1) + pltpu.roll(sums[2], BS - 1, axis=1)

    def at_lanes(tile, count):
        return pl.ds(pl.multiple_of(half * tile, half), count * half)

    def mover(out, into, send, recv):
        def outgoing(g, i):
            k = BATCH * g + i
            return pltpu.make_async_remote_copy(
                src_ref=out.at[k], dst_ref=into.at[gy], send_sem=send.at[k], recv_sem=recv.at[k],
                device_id=(gx, peer(g, i // 2, i % 2, 1)), device_id_type=MESH)

        def incoming(g, i):
            k = BATCH * g + i
            source = peer(g, i // 2, i % 2, -1)
            return pltpu.make_async_remote_copy(
                src_ref=out.at[k], dst_ref=into.at[source], send_sem=send.at[k], recv_sem=recv.at[k],
                device_id=(gx, source), device_id_type=MESH)

        def each(g, act):
            for i in range(BATCH):
                if i == BATCH - 2:
                    pl.when(g < HELD // BATCH - 1)(lambda: act(g, BATCH - 2))
                else:
                    act(g, i)

        def start(g):
            each(g, lambda g, i: outgoing(g, i).start())

        def finish(g, carry):
            def wait(g, i):
                outgoing(g, i).wait_send()
                incoming(g, i).wait_recv()

            each(g, wait)
            return carry

        return start, finish

    def choose(g, carry):
        for i in range(BATCH):
            chosen[BATCH * g + i] = slot_of(g, i // 2, i % 2)
        return carry

    lax.fori_loop(0, HELD // BATCH, choose, 0)
    start_inner, finish_inner = mover(inner_out, inner_in, inner_ss, inner_rs)
    start_shell, finish_shell = mover(shell_out, shell_in, shell_ss, shell_rs)

    def inner_batch(g, carry):
        def gather(pair, inner):
            two = [chosen[BATCH * g + 2 * pair + dc] for dc in range(2)]
            for x in range(BS):
                both = jnp.concatenate([pool[two[0], x], pool[two[1], x]], axis=0)
                inner_tiles[x % 2, x // 2, pl.ds(pl.multiple_of(2 * BS * pair, 2 * BS), 2 * BS), :] = both.astype(BF16)
            return inner

        lax.fori_loop(0, BATCH // 2, gather, 0)
        slots = [chosen[BATCH * g + i] for i in range(BATCH)]

        total = product(
            lambda d, odd, first, lanes: inner_tiles[odd, first : first + 3, :, lanes],
            inner_bands, 3, [pl.ds(half * q, 2 * half) for q in range(3)])
        for b in range(BATCH):
            parts = []
            for x in range(6):
                keep = between([mask[slots[b], x + 1, :, t * half : (t + 1) * half] for t in range(4)])
                at = (x % 2) * half
                for q in range(3):
                    value = total[(3 * q + x // 2) * BATCH + b, :, at : at + half]
                    parts.append((value + bias) * keep[q])
            packed = []
            for m in range(4):
                for j in range(3):
                    packed.append(jnp.where(edge_row, turn(parts[4 * m + 3], 6 - 2 * j), parts[4 * m + j]))
            for m, part in enumerate(packed + parts[16:]):
                inner_out[BATCH * g + b, m] = part.astype(BF16)
        start_inner(g)
        return carry

    def block_rows(slot, ox, x):
        views = []
        for oy in range(3):
            around = [nbr_ref[9 * ox + 3 * oy + oz, 0, slot] for oz in range(3)]
            parts = [pool[around[0], x, :, 3 * half : 4 * half]]
            parts += [pool[around[1], x, :, t * half : (t + 1) * half] for t in range(4)]
            parts += [pool[around[2], x, :, 0:half]]
            views.append([jnp.where(low_half, parts[t + 1], parts[t]) for t in range(5)])
        before, here, after = views
        return (
            [jnp.where(last_row, b, h) for b, h in zip(before, here)],
            here,
            [jnp.where(first_row, a, h) for a, h in zip(after, here)],
        )

    def shell_batch(g, carry):
        def assemble(pair, inner):
            two = [chosen[BATCH * g + 2 * pair + dc] for dc in range(2)]
            for xx in range(BS + 2):
                ox = 0 if xx == 0 else (2 if xx == BS + 1 else 1)
                x = (xx - 1) % BS
                first, second = block_rows(two[0], ox, x), block_rows(two[1], ox, x)
                for d in range(3):
                    for t in range(5):
                        both = jnp.concatenate([first[d][t], second[d][t]], axis=0)
                        tiles[
                            d, xx % 2, xx // 2, pl.ds(pl.multiple_of(2 * BS * pair, 2 * BS), 2 * BS), t * half : (t + 1) * half
                        ] = both.astype(BF16)
            return inner

        lax.fori_loop(0, BATCH // 2, assemble, 0)
        slots = [chosen[BATCH * g + i] for i in range(BATCH)]

        def columns(step, inner):
            total = product(
                lambda d, odd, first, lanes: tiles[d, odd, first : first + 4, :, lanes],
                bands, 4, [at_lanes(GROUP * step + i, 2) for i in range(GROUP)])
            for i in range(GROUP):
                here = at_lanes(GROUP * step + i, 1)
                for b in range(BATCH):
                    for x in range(BS):
                        at = (x % 2) * half
                        part = total[(4 * i + x // 2) * BATCH + b, :, at : at + half] + bias
                        stage[b, x, :, here] = part * mask[slots[b], x, :, here]
            return inner

        lax.fori_loop(0, 4 // GROUP, columns, 0)

        def pack(b, inner):
            pack_shell(stage, b, shell_out, BATCH * g + b)
            return inner

        lax.fori_loop(0, BATCH, pack, 0)
        start_shell(g)
        return carry

    lax.fori_loop(0, EARLY, inner_batch, 0)
    take_y()
    send_x()
    lax.fori_loop(EARLY, HELD // BATCH, inner_batch, 0)
    build_bands(w_ref, bands, (1, 0, 3, 2), False)
    take_x()
    lax.fori_loop(0, HELD // BATCH, shell_batch, 0)
    inner_in[gy] = inner_out[HELD - 2]
    shell_in[gy] = shell_out[HELD - 2]
    settle_y()
    settle_x()
    lax.fori_loop(0, HELD // BATCH, finish_inner, 0)
    lax.fori_loop(0, HELD // BATCH, finish_shell, 0)

    def place(r, carry):
        source = order_ref[0, r]
        for side, x in enumerate((0, BS - 1)):
            for t in range(4):
                out_ref[r, x, :, t * half : (t + 1) * half] = shell_in[source, 4 * side + t]
        arrived = [inner_in[source, m].astype(F32) for m in range(INNER)]
        strips = outer_y(shell_in, source)
        middle = []
        for i in range(18):
            if i >= 16:
                tile = arrived[i - 4]
            elif i % 4 < 3:
                tile = arrived[3 * (i // 4) + i % 4]
            else:
                first, second, third = arrived[3 * (i // 4) : 3 * (i // 4) + 3]
                tile = jnp.where(row <= 2, turn(first, 2), jnp.where(row <= 4, turn(second, 4), turn(third, 6)))
            middle.append(jnp.where(edge_row, strips[i], tile))
        for x in range(6):
            ends = shell_in[source, 8 + x].astype(F32)
            for t, tile in enumerate(joined(ends, middle[3 * x : 3 * x + 3])):
                out_ref[r, x + 1, :, t * half : (t + 1) * half] = tile.astype(BF16)
        return carry

    lax.fori_loop(0, OUT, place, 0)


def on_device(features, occupancy, neighbors, face_lists, face_relays, send_slots, receive_order, weights, channel_bias):
    block = (BS, BS, LANES)
    out = pl.pallas_call(
        kernel,
        out_shape=jax.ShapeDtypeStruct((OUT,) + block, BF16),
        in_specs=[pl.BlockSpec(memory_space=pltpu.HBM)] * 9,
        out_specs=pl.BlockSpec(memory_space=pltpu.VMEM),
        scratch_shapes=[
            pltpu.SMEM((1, 2 * FACE), jnp.int32),
            pltpu.SMEM((1, 2 * FACE), jnp.int32),
            pltpu.SMEM((1, HELD), jnp.int32),
            pltpu.SMEM((1, OUT), jnp.int32),
            pltpu.SMEM((27, 1, HELD), jnp.int32),
            pltpu.VMEM((occupancy.shape[-1], 1, HELD), jnp.int32),
            pltpu.VMEM(weights.shape, BF16),
            pltpu.VMEM((1, C), F32),
            pltpu.SMEM((HELD,), jnp.int32),
            pltpu.VMEM((HELD,) + block, BF16),
            pltpu.VMEM((POOL,) + block, F32),
            pltpu.VMEM((HELD,) + block, F32),
            pltpu.VMEM((HELD, LANES), F32),
            pltpu.VMEM((2, 4, BATCH * BS, LANES), BF16),
            pltpu.VMEM((3, 16 * C, 4 * C), BF16),
            pltpu.VMEM((3, 2, 5, BATCH * BS, LANES + 2 * C), BF16),
            pltpu.VMEM((3, 16 * C, 4 * C), BF16),
            pltpu.VMEM((BATCH,) + block, F32),
            pltpu.VMEM((HELD, INNER, BS, 2 * C), BF16),
            pltpu.VMEM((HELD, INNER, BS, 2 * C), BF16),
            pltpu.VMEM((HELD, SHELL, BS, 2 * C), BF16),
            pltpu.VMEM((HELD, SHELL, BS, 2 * C), BF16),
            pltpu.VMEM((2 * FACE, SHELL, BS, 2 * C), BF16),
            pltpu.VMEM((2 * FACE, SHELL, BS, 2 * C), BF16),
            pltpu.VMEM((2 * FACE, SHELL, BS, 2 * C), BF16),
            pltpu.VMEM((2 * FACE, SHELL, BS, 2 * C), BF16),
            pltpu.SemaphoreType.DMA((8,)),
            pltpu.SemaphoreType.DMA((4,)),
            pltpu.SemaphoreType.DMA((2 * FACE,)),
            pltpu.SemaphoreType.DMA((2 * FACE,)),
            pltpu.SemaphoreType.DMA((2 * FACE,)),
            pltpu.SemaphoreType.DMA((2 * FACE,)),
            pltpu.SemaphoreType.DMA((HELD,)),
            pltpu.SemaphoreType.DMA((HELD,)),
            pltpu.SemaphoreType.DMA((HELD,)),
            pltpu.SemaphoreType.DMA((HELD,)),
        ],
        compiler_params=pltpu.CompilerParams(
            collective_id=0, has_side_effects=True, vmem_limit_bytes=50 << 20
        ),
    )(
        *(
            pltpu.with_memory_space_constraint(operand, pltpu.HBM)
            for operand in (
                face_lists[0],
                face_relays[0],
                send_slots[0, :, :, 0],
                receive_order[0],
                jnp.transpose(neighbors[0], (2, 0, 1)),
                jnp.transpose(occupancy[0], (2, 0, 1)),
                features[0, 0],
                weights,
                channel_bias.reshape(1, C),
            )
        )
    )
    return out[None, None]


def solution(mesh):
    in_specs = (
        P("gx", "gy", None, None, None, None),
        P("gx", "gy", None, None),
        P("gx", "gy", None, None),
        P("gx", "gy", None),
        P("gx", "gy", None),
        P("gx", "gy", None, None),
        P("gx", "gy", None),
        P(),
        P(),
    )
    out_specs = P("gx", "gy", None, None, None, None)
    return jax.shard_map(
        on_device, mesh=mesh, in_specs=in_specs, out_specs=out_specs, check_vma=False
    )
```
